32 devices in a mesh: angle: 8 (over z, y), tile: 2 (over x), half: 2 (over core).
Axes of the slice: x: 2, y: 2, z: 4, core: 2. Of those that a mesh axis runs over, the one named last changes fastest.
Arguments:
- projection: float32 [16, 2, 64, 256], P(('angle', 'half'), None, 'tile'), may hold values from -6 to 6
- multiplier: float32 [16, 2, 64, 256], P(('angle', 'half'), None, 'tile'), may hold values from -3 to 3
- reprojection: float32 [16, 64, 256], P(('angle', 'half'), 'tile'), may hold values from -6 to 6
- intensity: bfloat16 [16, 64, 64, 128], P(('angle', 'half'), 'tile'), may hold values from 0 to 4
- row_start: int32 [16, 64], P(('angle', 'half'), 'tile'), may hold values from -32 to 0
- column_start: int32 [16, 64], P(('angle', 'half'), 'tile'), may hold values from 0 to 128
- probe_field: float32 [2, 64, 128], replicated, may hold values from -6 to 6
- probe_mask: int32 [64, 128], replicated, may hold values 0 or 1
- weights: bfloat16 [16, 2, 4, 128, 512], P('angle'), may hold values from -0.125 to 0.125
- ray_blocks: int32 [16, 2, 4], P('angle'), may hold values from 0 to 127, as said below
- ray_counts: int32 [16, 2], P('angle'), may hold values from 1 to 4, as said below
- volume: float32 [128, 64, 512], P('angle', ('tile', 'half')), may hold values from -6 to 6
Outputs:
- updated_projection: float32 [16, 2, 64, 256], P(('angle', 'half'), None, 'tile')
- volume_new: float32 [128, 64, 512], P('angle', ('tile', 'half'))
- multiplier_new: float32 [16, 2, 64, 256], P('angle', None, ('tile', 'half'))
The draws below stay inside these ranges and needn't reach their ends.
Inputs may be any that keep to these rules, and one draw needn't show every extreme that they name: A ray block uses its first ray_counts weight tiles; some ray block uses all 4. `ray_blocks`: slots at or past a ray block's count are not used. Split the angles into aligned groups of 2 and the pixel blocks into aligned groups of 16: the 16 slots of one angle group name blocks of one block group at most 2 times, and exactly 2 times for some block group.
All inputs are finite; a program needn't handle non-finite values.
Results may differ from the reference program's by a relative error of at most 0.008.
Values may be sent and summed in bfloat16 or wider, within the bound.
A program may use at most 64 MiB of HBM per device.

```python
import jax
import jax.numpy as jnp
from jax import lax

PR = 64
PC = 128
NW = 256
PIX = 512
RB = 128
CMAX = 4
BAND = 32
P_DEV = 32
HALO = 32
ANGLES = 16
ANG_T = 2
SLICES = 64
NRB = 2
NPB = 128
CAP = 2
PATCHES = 64


def draw_ray_counts(key, part):
    first, second, third = jax.random.split(key, 3)
    base = jax.random.randint(first, (ANGLES * NRB,), 1, CMAX + 1)
    heavy = jax.random.randint(second, (ANGLES * NRB,), 0, 3)
    counts = jnp.where(heavy == 0, CMAX, base)
    position = jax.random.randint(third, (), 0, ANGLES * NRB)
    counts = counts.at[position].set(CMAX)
    return counts.reshape(ANGLES, NRB).astype(jnp.int32)


def draw_ray_blocks(key, part):
    groups = ANGLES // ANG_T
    owned = NPB // groups
    slot_count = ANG_T * NRB * CMAX
    base = jax.random.fold_in(key, 7)
    group_keys = jax.random.split(base, groups)

    def one_group(group_key):
        first, second, third, fourth = jax.random.split(group_key, 4)
        leader = jax.random.randint(first, (), 0, groups)
        others = (leader + 1 + jnp.arange(groups - 1, dtype=jnp.int32)) % groups
        others = jax.random.permutation(second, jnp.repeat(others, CAP))
        owners = jnp.concatenate([jnp.full((CAP,), leader, jnp.int32), others])[:slot_count]
        owners = jax.random.permutation(third, owners)
        inside = jax.random.randint(fourth, (slot_count,), 0, owned)
        return (owners * owned + inside).astype(jnp.int32)
    blocks = jax.vmap(one_group)(group_keys)
    return blocks.reshape(ANGLES, NRB, CMAX).astype(jnp.int32)


def set_ends(drawn, key, smallest, top_value):
    place = [jax.random.randint(jax.random.fold_in(key, axis), (), 0, length) for axis, length in enumerate(drawn.shape)]
    main_axis = drawn.shape.index(max(drawn.shape))
    neighbour = place[:main_axis] + [(place[main_axis] + 1) % drawn.shape[main_axis]] + place[main_axis + 1:]
    return drawn.at[tuple(place)].set(smallest).at[tuple(neighbour)].set(top_value)


def block_scale(stream_key, shape, cuts, low, high):
    def one(dim, blocks):
        draws = jax.random.uniform(jax.random.fold_in(jax.random.fold_in(stream_key, 6), dim), (blocks,), jnp.float32, low / len(cuts), high / len(cuts))
        return jnp.repeat(jnp.exp(draws), shape[dim] // blocks).reshape((-1,) + (1,) * (len(shape) - dim - 1))

    factor_of = one(*cuts[0])
    for cut in cuts[1:]:
        factor_of = factor_of * one(*cut)
    return factor_of


def centred(rng, extent, scale, most, cuts=(), kind=jnp.bfloat16):
    entries = jax.random.normal(rng, extent, jnp.float32) * scale
    if len(cuts) > 0:
        entries = block_scale(rng, extent, cuts, -0.22, 0.18) * entries
    return jnp.clip(entries, min=-most, max=most).astype(kind)


def setup_inputs(seed: int = 0) -> dict:
    streams_of = jax.random.split(jax.random.key(seed), 13)
    return {
        "projection": centred(streams_of[0], (ANGLES, 2, SLICES, NW), 1.0, 6.0, ((0, 16), (2, 2)), jnp.float32),
        "multiplier": centred(streams_of[1], (ANGLES, 2, SLICES, NW), 0.5, 3.0, ((0, 16), (2, 2)), jnp.float32),
        "reprojection": centred(streams_of[2], (ANGLES, SLICES, NW), 1.0, 6.0, ((0, 16), (1, 2)), jnp.float32),
        "intensity": jnp.clip(4.0 * jax.random.uniform(streams_of[3], (ANGLES, PATCHES, PR, PC), jnp.float32) ** block_scale(streams_of[3], (ANGLES, PATCHES, PR, PC), ((0, 16), (1, 2)), -0.2, 0.2), 0.0, 4.0).astype(jnp.bfloat16),
        "row_start": set_ends(jax.random.randint(streams_of[4], (ANGLES, PATCHES), 0 - HALO, BAND + HALO - PR + 1), jax.random.fold_in(streams_of[4], 1), 0 - HALO, BAND + HALO - PR).astype(jnp.int32),
        "column_start": set_ends(jax.random.randint(streams_of[5], (ANGLES, PATCHES), 0, NW - PC + 1), jax.random.fold_in(streams_of[5], 1), 0, NW - PC).astype(jnp.int32),
        "probe_field": centred(streams_of[6], (2, PR, PC), 1.0, 6.0, (), jnp.float32),
        "probe_mask": set_ends((jax.random.randint(streams_of[7], (PR, PC), 0, 4) < 3).astype(jnp.int32), jax.random.fold_in(streams_of[7], 1), 0, 1),
        "weights": centred(streams_of[8], (ANGLES, NRB, CMAX, RB, PIX), (CMAX * PIX) ** -0.5, 0.125, ((0, 8),)),
        "ray_blocks": draw_ray_blocks(jax.random.fold_in(streams_of[12], 71), 0),
        "ray_counts": draw_ray_counts(jax.random.fold_in(streams_of[12], 71), 0),
        "volume": centred(streams_of[11], (NPB, SLICES, PIX), 1.0, 6.0, ((0, 8), (1, 4)), jnp.float32),
    }


penalty = 0.5
descent = 0.25
volume_step = 1.0
damping = 0.1
highest = lax.Precision.HIGHEST

def to_half(values):
    return lax.optimization_barrier(values.astype(jnp.bfloat16)).astype(jnp.float32)

def ptycho_angle(inputs, masked_probe):
    object_band, mult_band, prior_band, measured, rows_in, columns_in = inputs
    padded = jnp.pad(object_band, ((0, 0), (HALO, HALO), (0, 0)))
    offsets = jnp.arange(PATCHES, dtype=jnp.int32) // P_DEV * BAND + rows_in.astype(jnp.int32) + HALO
    zero_index = jnp.zeros((), jnp.int32)

    def cutout(first_row, first_column):
        return lax.dynamic_slice(padded, (zero_index, first_row, first_column), (2, PR, PC))
    pieces = jax.vmap(cutout)(offsets, columns_in.astype(jnp.int32))
    wave_real = masked_probe[0] * pieces[:, 0] - masked_probe[1] * pieces[:, 1]
    wave_imag = masked_probe[0] * pieces[:, 1] + masked_probe[1] * pieces[:, 0]
    far = jnp.fft.fft2(lax.complex(wave_real, wave_imag), norm='ortho')
    far_real = jnp.real(far)
    far_imag = jnp.imag(far)
    factor = 1.0 - jnp.sqrt(measured.astype(jnp.float32)) / jnp.sqrt(far_real * far_real + far_imag * far_imag + 1.0)
    back = jnp.fft.ifft2(lax.complex(far_real * factor, far_imag * factor), norm='ortho')
    back_real = jnp.real(back)
    back_imag = jnp.imag(back)
    grad_real = masked_probe[0] * back_real + masked_probe[1] * back_imag
    grad_imag = masked_probe[0] * back_imag - masked_probe[1] * back_real
    patch_grads = jnp.stack([grad_real, grad_imag], axis=1)

    def accumulate(total, item):
        values, first_row, first_column = item
        window = lax.dynamic_slice(total, (zero_index, first_row, first_column), (2, PR, PC))
        return (lax.dynamic_update_slice(total, window + values, (zero_index, first_row, first_column)), None)
    total, unused = lax.scan(accumulate, jnp.zeros_like(padded), (patch_grads, offsets, columns_in.astype(jnp.int32)))
    gradient = total[:, HALO:HALO + SLICES]
    holder = jnp.stack([jnp.ones_like(prior_band), prior_band], axis=0)
    return object_band - descent * (gradient + penalty * (object_band - holder) + mult_band)

def live_slots(block_count):
    return (jnp.arange(CMAX, dtype=jnp.int32)[None, :] < block_count[:, None]).astype(jnp.float32)

def project(field, weights, ray_blocks, ray_counts):

    def one_angle(inputs):
        tile_weights, block_index, block_count = inputs
        masked = tile_weights.astype(jnp.float32) * live_slots(block_count)[:, :, None, None]
        picked = field[block_index]
        result = jnp.einsum('kcrp,kcsp->skr', masked, picked, precision=highest)
        return result.reshape(SLICES, NW)
    return lax.map(one_angle, (weights, ray_blocks, ray_counts))

def reference(projection, multiplier, reprojection, intensity, row_start, column_start, probe_field, probe_mask, weights, ray_blocks, ray_counts, volume):
    masked_probe = probe_field * probe_mask.astype(jnp.float32)[None]
    updated = lax.map(lambda inputs: ptycho_angle(inputs, masked_probe), (projection, multiplier, reprojection, intensity, row_start, column_start))
    target = updated[:, 1] + multiplier[:, 1] / penalty
    sinogram = project(to_half(volume), weights, ray_blocks, ray_counts)
    residual = to_half(sinogram - target)

    def spread_angle(total, inputs):
        tile_weights, block_index, block_count, residual_angle = inputs
        masked = tile_weights.astype(jnp.float32) * live_slots(block_count)[:, :, None, None]
        spread = jnp.einsum('kcrp,skr->kcsp', masked, residual_angle.reshape(SLICES, NRB, RB), precision=highest)
        return (total.at[block_index.reshape(-1)].add(spread.reshape(NRB * CMAX, SLICES, PIX)), None)
    block_gradient, unused = lax.scan(spread_angle, jnp.zeros((NPB, SLICES, PIX), jnp.float32), (weights, ray_blocks, ray_counts, residual))
    volume_new = volume - volume_step * (block_gradient + damping * volume)
    fresh = project(to_half(volume_new), weights, ray_blocks, ray_counts)
    fresh_holder = jnp.stack([jnp.ones_like(fresh), fresh], axis=1)
    multiplier_new = multiplier + penalty * (updated - fresh_holder)
    return (updated, volume_new, multiplier_new)
```

```python
import jax
import jax.numpy as jnp
import numpy as np
from jax import lax
from jax.experimental import pallas as pl
from jax.experimental.pallas import tpu as pltpu
from jax.sharding import PartitionSpec as P

PR = 64
PC = 128
NW = 256
PIX = 512
RB = 128
CMAX = 4
HALO = 32
NRB = 2


penalty = 0.5
descent = 0.25
volume_step = 1.0
damping = 0.1
highest = lax.Precision.HIGHEST


def neighbours(axis):
    devices = lax.axis_size(axis)
    up = [(i, i + 1) for i in range(devices - 1)]
    return up, [(j, i) for i, j in up]


def dft_blocks(sign):
    def table(length):
        counter = np.arange(length)
        phase = (counter[:, None] * counter[None, :] % length) * (2.0 * np.pi / length)
        return np.cos(phase) / np.sqrt(length), sign * np.sin(phase) / np.sqrt(length)

    row_cos, row_sin = table(PR)
    col_cos, col_sin = table(PC)
    left = np.block([[row_cos, -row_sin], [row_sin, row_cos]])
    right = np.block([[col_cos, col_sin], [-col_sin, col_cos]])
    return left.astype(np.float32), right.astype(np.float32)


CHUNK = 4


def ptycho_kernel(
    rows_ref, cols_ref, before_ref, own_ref, after_ref, measured_ref, field_ref, mask_ref,
    left_f_ref, right_f_ref, left_b_ref, right_b_ref,
    top_ref, mid_ref, bottom_ref, ext_ref, acc_ref, wave_ref,
):
    band = own_ref.shape[2]
    lanes = [slice(0, PC), slice(PC, NW)]
    for side in range(2):
        ext_ref[:, side, :HALO] = before_ref[0, :, :, lanes[side]]
        ext_ref[:, side, HALO : HALO + band] = own_ref[0, :, :, lanes[side]]
        ext_ref[:, side, HALO + band :] = after_ref[0, :, :, lanes[side]]
    acc_ref[...] = jnp.zeros_like(acc_ref)
    half = jnp.bfloat16
    mask = mask_ref[...].astype(jnp.float32)
    wave_ref[0] = field_ref[0] * mask
    wave_ref[1] = field_ref[1] * mask

    lane = lax.broadcasted_iota(jnp.int32, (PR, PC), 1)

    def dot(a, b):
        return jnp.dot(a, b, preferred_element_type=jnp.float32)

    def step(chunk, carry):
        waves = []
        places = []
        for j in range(CHUNK):
            p = chunk * CHUNK + j
            row = rows_ref[0, p] + HALO
            col = cols_ref[0, p]
            places.append((row, col))
            back_shift = lax.rem(NW - col, PC)

            def window(channel):
                near = pltpu.roll(ext_ref[channel, 0, pl.ds(row, PR), :], back_shift, 1)
                next_ = pltpu.roll(ext_ref[channel, 1, pl.ds(row, PR), :], back_shift, 1)
                return jnp.where(lane + col < PC, near, next_)

            o_re = window(0)
            o_im = window(1)
            p_re, p_im = wave_ref[0], wave_ref[1]
            waves.append(
                jnp.concatenate([p_re * o_re - p_im * o_im, p_re * o_im + p_im * o_re], axis=0)
            )
        wide = jnp.concatenate(waves, axis=1).astype(half)
        first = dot(left_f_ref[...], wide).astype(half)
        tall = jnp.concatenate(
            [
                jnp.concatenate(
                    [first[:PR, j * PC : (j + 1) * PC], first[PR:, j * PC : (j + 1) * PC]], axis=1
                )
                for j in range(CHUNK)
            ],
            axis=0,
        )
        far = dot(tall, right_f_ref[...])
        f_re, f_im = far[:, :PC], far[:, PC:]
        measured = measured_ref[0, pl.ds(chunk * CHUNK, CHUNK)].astype(jnp.float32)
        measured = measured.reshape(CHUNK * PR, PC)
        factor = 1.0 - jnp.sqrt(measured) * lax.rsqrt(f_re * f_re + f_im * f_im + 1.0)
        scaled = jnp.concatenate([f_re * factor, f_im * factor], axis=1).astype(half)
        second = dot(scaled, right_b_ref[...]).astype(half)
        wide = jnp.concatenate(
            [
                jnp.concatenate(
                    [second[j * PR : (j + 1) * PR, :PC], second[j * PR : (j + 1) * PR, PC:]], axis=0
                )
                for j in range(CHUNK)
            ],
            axis=1,
        )
        back = dot(left_b_ref[...], wide)
        for j in range(CHUNK):
            row, col = places[j]
            b_re = back[:PR, j * PC : (j + 1) * PC]
            b_im = back[PR:, j * PC : (j + 1) * PC]
            p_re, p_im = wave_ref[0], wave_ref[1]
            shift = lax.rem(col, PC)
            for channel, values in ((0, p_re * b_re + p_im * b_im), (1, p_re * b_im - p_im * b_re)):
                values = pltpu.roll(values, shift, 1)
                acc_ref[channel, 0, pl.ds(row, PR), :] += jnp.where(lane >= col, values, 0.0)
                acc_ref[channel, 1, pl.ds(row, PR), :] += jnp.where(lane >= col, 0.0, values)
        return carry

    lax.fori_loop(0, rows_ref.shape[1] // CHUNK, step, 0)
    for side in range(2):
        top_ref[0, :, :, lanes[side]] = acc_ref[:, side, :HALO]
        mid_ref[0, :, :, lanes[side]] = acc_ref[:, side, HALO : HALO + band]
        bottom_ref[0, :, :, lanes[side]] = acc_ref[:, side, HALO + band :]


def patch_sums(before, own, after, rows, cols, measured, field, mask):
    band = own.shape[2]
    left_f, right_f = dft_blocks(-1.0)
    left_b, right_b = dft_blocks(1.0)
    tables = [jnp.asarray(m, jnp.bfloat16) for m in (left_f, right_f, left_b, right_b)]
    vmem = pl.BlockSpec(memory_space=pltpu.VMEM)
    smem = pl.BlockSpec(memory_space=pltpu.SMEM)
    rim = jax.ShapeDtypeStruct(before.shape, jnp.float32)
    ext_rows = band + 2 * HALO
    return pl.pallas_call(
        ptycho_kernel,
        out_shape=(rim, jax.ShapeDtypeStruct(own.shape, jnp.float32), rim),
        in_specs=[smem, smem] + [vmem] * 10,
        out_specs=(vmem, vmem, vmem),
        scratch_shapes=[
            pltpu.VMEM((2, NW // PC, ext_rows, PC), jnp.float32),
            pltpu.VMEM((2, NW // PC, ext_rows, PC), jnp.float32),
            pltpu.VMEM((2, PR, PC), jnp.float32),
        ],
        cost_estimate=pl.CostEstimate(
            flops=2000000000, bytes_accessed=2000000, transcendentals=500000
        ),
    )(rows, cols, before, own, after, measured, field, mask, *tables)


def swap_half(value):
    return lax.ppermute(value, "half", [(0, 1), (1, 0)])


def to_slices(value):
    side = lax.axis_index("half")
    rows = value.shape[2] // 2
    low, high = value[:, :, :rows], value[:, :, rows:]
    kept = jnp.where(side == 0, low, high)
    other = swap_half(jnp.where(side == 0, high, low))
    return jnp.concatenate(
        [jnp.where(side == 0, kept, other), jnp.where(side == 0, other, kept)], axis=0
    )


def shards(
    projection,
    multiplier,
    reprojection,
    intensity,
    row_start,
    column_start,
    probe_field,
    probe_mask,
    weights,
    ray_blocks,
    ray_counts,
    volume,
):
    up, down = neighbours("tile")
    band_rows = projection.shape[2]
    before = lax.ppermute(projection[:, :, band_rows - HALO :], "tile", up)
    after = lax.ppermute(projection[:, :, :HALO], "tile", down)
    moved_mult = to_slices(multiplier)
    top, gradient, bottom = patch_sums(
        before, projection, after, row_start, column_start, intensity, probe_field, probe_mask
    )
    from_above = lax.ppermute(bottom, "tile", up)
    from_below = lax.ppermute(top, "tile", down)
    if band_rows == HALO:
        gradient = gradient + from_above + from_below
    else:
        gradient = gradient.at[:, :, :HALO].add(from_above)
        gradient = gradient.at[:, :, band_rows - HALO :].add(from_below)
    holder = jnp.stack([jnp.ones_like(reprojection), reprojection], axis=1)
    updated = projection - descent * (gradient + penalty * (projection - holder) + multiplier)
    moved = jnp.concatenate([to_slices(updated), moved_mult], axis=1)
    target = moved[:, 1] + moved[:, 3] / penalty
    angle_count = weights.shape[0]
    slice_rows = volume.shape[1]
    own_blocks = volume.shape[0]
    live = lax.iota(jnp.int32, CMAX)[None, None, :] < ray_counts[:, :, None]
    groups = lax.axis_size("angle")
    slot_count = angle_count * NRB * CMAX
    capacity = max(2, -(-slot_count // groups))
    flat_ids = ray_blocks.reshape(slot_count)
    owners = flat_ids // own_blocks
    local_ids = flat_ids % own_blocks
    owner_hits = (owners[:, None] == lax.iota(jnp.int32, groups)[None, :]).astype(jnp.int32)
    slot_ranks = jnp.sum((jnp.cumsum(owner_hits, axis=0) - 1) * owner_hits, axis=1)
    slot_place = owners * capacity + slot_ranks
    requests = (
        jnp.zeros((groups * capacity,), jnp.int32)
        .at[slot_place]
        .set(local_ids)
        .reshape(groups, capacity)
    )
    wanted = lax.all_to_all(requests, "angle", split_axis=0, concat_axis=0, tiled=True).reshape(
        groups * capacity
    )
    live_half = live.astype(jnp.bfloat16)[:, :, :, None, None]

    def fetch_blocks(field):
        replies = field.astype(jnp.bfloat16)[wanted].reshape(groups, capacity, slice_rows, PIX)
        arrived = lax.all_to_all(replies, "angle", split_axis=0, concat_axis=0, tiled=True)
        picked = arrived.reshape(groups * capacity, slice_rows, PIX)[slot_place]
        picked = picked.reshape(angle_count, NRB, CMAX, slice_rows, PIX) * live_half
        result = jnp.einsum(
            "tkcrp,tkcsp->tskr", weights, picked, preferred_element_type=jnp.float32
        )
        return result.reshape(angle_count, slice_rows, NW)

    sinogram = fetch_blocks(volume)
    residual = (sinogram - target).astype(jnp.bfloat16).reshape(angle_count, slice_rows, NRB, RB)
    spread = (
        jnp.einsum("tkcrp,tskr->tkcsp", weights, residual, preferred_element_type=jnp.float32)
        * live.astype(jnp.float32)[:, :, :, None, None]
    )
    outgoing = (
        jnp.zeros((groups * capacity, slice_rows, PIX), jnp.float32)
        .at[slot_place]
        .set(spread.reshape(slot_count, slice_rows, PIX))
    )
    incoming = lax.all_to_all(
        outgoing.reshape(groups, capacity, slice_rows, PIX).astype(jnp.bfloat16),
        "angle",
        split_axis=0,
        concat_axis=0,
        tiled=True,
    ).astype(jnp.float32)
    placing = (wanted[:, None] == lax.iota(jnp.int32, own_blocks)[None, :]).astype(jnp.float32)
    block_grad = jnp.einsum(
        "nj,nsp->jsp",
        placing,
        incoming.reshape(groups * capacity, slice_rows, PIX),
        precision=highest,
    )
    new_volume = volume - volume_step * (block_grad + damping * volume)
    fresh = fetch_blocks(new_volume)
    fresh_holder = jnp.stack([jnp.ones_like(fresh), fresh], axis=1)
    new_multiplier = moved[:, 2:] + penalty * (moved[:, :2] - fresh_holder)
    return (updated, new_volume, new_multiplier)


def solution(mesh):
    return jax.shard_map(
        shards,
        mesh=mesh,
        in_specs=(
            P(("angle", "half"), None, "tile", None),
            P(("angle", "half"), None, "tile", None),
            P(("angle", "half"), "tile", None),
            P(("angle", "half"), "tile", None, None),
            P(("angle", "half"), "tile"),
            P(("angle", "half"), "tile"),
            P(),
            P(),
            P("angle", None, None, None, None),
            P("angle", None, None),
            P("angle", None),
            P("angle", ("tile", "half"), None),
        ),
        out_specs=(
            P(("angle", "half"), None, "tile", None),
            P("angle", ("tile", "half"), None),
            P("angle", None, ("tile", "half"), None),
        ),
        check_vma=False,
    )
```

```python
import functools

import jax
import jax.numpy as jnp
import numpy as np
from jax import lax
from jax.experimental import pallas as pl
from jax.experimental.pallas import tpu as pltpu
from jax.sharding import PartitionSpec as P

PR = 64
PC = 128
NW = 256
PIX = 512
RB = 128
CMAX = 4
HALO = 32
NRB = 2


penalty = 0.5
descent = 0.25
volume_step = 1.0
damping = 0.1


def neighbours(axis):
    devices = lax.axis_size(axis)
    up = [(i, i + 1) for i in range(devices - 1)]
    return up, [(j, i) for i, j in up]


def dft_blocks(sign):
    def table(length):
        counter = np.arange(length)
        phase = (counter[:, None] * counter[None, :] % length) * (2.0 * np.pi / length)
        return np.cos(phase) / np.sqrt(length), sign * np.sin(phase) / np.sqrt(length)

    row_cos, row_sin = table(PR)
    col_cos, col_sin = table(PC)
    left = np.block([[row_cos, -row_sin], [row_sin, row_cos]])
    right = np.block([[col_cos, col_sin], [-col_sin, col_cos]])
    return left.astype(np.float32), right.astype(np.float32)


CHUNK = 4


def ptycho_kernel(
    rows_ref, cols_ref, before_ref, own_ref, after_ref, measured_ref, field_ref, mask_ref,
    left_f_ref, right_f_ref, left_b_ref, right_b_ref,
    top_ref, mid_ref, bottom_ref, ext_ref, acc_ref, wave_ref,
):
    band = own_ref.shape[2]
    lanes = [slice(0, PC), slice(PC, NW)]
    for side in range(2):
        ext_ref[:, side, :HALO] = before_ref[0, :, :, lanes[side]]
        ext_ref[:, side, HALO : HALO + band] = own_ref[0, :, :, lanes[side]]
        ext_ref[:, side, HALO + band :] = after_ref[0, :, :, lanes[side]]
    acc_ref[...] = jnp.zeros_like(acc_ref)
    half = jnp.bfloat16
    mask = mask_ref[...].astype(jnp.float32)
    wave_ref[0] = field_ref[0] * mask
    wave_ref[1] = field_ref[1] * mask

    lane = lax.broadcasted_iota(jnp.int32, (PR, PC), 1)

    def dot(a, b):
        return jnp.dot(a, b, preferred_element_type=jnp.float32)

    def step(chunk, carry):
        waves = []
        places = []
        for j in range(CHUNK):
            p = chunk * CHUNK + j
            row = rows_ref[0, p] + HALO
            col = cols_ref[0, p]
            places.append((row, col))
            back_shift = lax.rem(NW - col, PC)

            def window(channel):
                near = pltpu.roll(ext_ref[channel, 0, pl.ds(row, PR), :], back_shift, 1)
                next_ = pltpu.roll(ext_ref[channel, 1, pl.ds(row, PR), :], back_shift, 1)
                return jnp.where(lane + col < PC, near, next_)

            o_re = window(0)
            o_im = window(1)
            p_re, p_im = wave_ref[0], wave_ref[1]
            waves.append(
                jnp.concatenate([p_re * o_re - p_im * o_im, p_re * o_im + p_im * o_re], axis=0)
            )
        wide = jnp.concatenate(waves, axis=1).astype(half)
        first = dot(left_f_ref[...], wide).astype(half)
        tall = jnp.concatenate(
            [
                jnp.concatenate(
                    [first[:PR, j * PC : (j + 1) * PC], first[PR:, j * PC : (j + 1) * PC]], axis=1
                )
                for j in range(CHUNK)
            ],
            axis=0,
        )
        far = dot(tall, right_f_ref[...])
        f_re, f_im = far[:, :PC], far[:, PC:]
        measured = measured_ref[0, pl.ds(chunk * CHUNK, CHUNK)].astype(jnp.float32)
        measured = measured.reshape(CHUNK * PR, PC)
        factor = 1.0 - jnp.sqrt(measured) * lax.rsqrt(f_re * f_re + f_im * f_im + 1.0)
        scaled = jnp.concatenate([f_re * factor, f_im * factor], axis=1).astype(half)
        second = dot(scaled, right_b_ref[...]).astype(half)
        wide = jnp.concatenate(
            [
                jnp.concatenate(
                    [second[j * PR : (j + 1) * PR, :PC], second[j * PR : (j + 1) * PR, PC:]], axis=0
                )
                for j in range(CHUNK)
            ],
            axis=1,
        )
        back = dot(left_b_ref[...], wide)
        for j in range(CHUNK):
            row, col = places[j]
            b_re = back[:PR, j * PC : (j + 1) * PC]
            b_im = back[PR:, j * PC : (j + 1) * PC]
            p_re, p_im = wave_ref[0], wave_ref[1]
            shift = lax.rem(col, PC)
            for channel, values in ((0, p_re * b_re + p_im * b_im), (1, p_re * b_im - p_im * b_re)):
                values = pltpu.roll(values, shift, 1)
                acc_ref[channel, 0, pl.ds(row, PR), :] += jnp.where(lane >= col, values, 0.0)
                acc_ref[channel, 1, pl.ds(row, PR), :] += jnp.where(lane >= col, 0.0, values)
        return carry

    lax.fori_loop(0, rows_ref.shape[1] // CHUNK, step, 0)
    for side in range(2):
        top_ref[0, :, :, lanes[side]] = acc_ref[:, side, :HALO]
        mid_ref[0, :, :, lanes[side]] = acc_ref[:, side, HALO : HALO + band]
        bottom_ref[0, :, :, lanes[side]] = acc_ref[:, side, HALO + band :]


def patch_sums(before, own, after, rows, cols, measured, field, mask):
    band = own.shape[2]
    left_f, right_f = dft_blocks(-1.0)
    left_b, right_b = dft_blocks(1.0)
    tables = [jnp.asarray(m, jnp.bfloat16) for m in (left_f, right_f, left_b, right_b)]
    vmem = pl.BlockSpec(memory_space=pltpu.VMEM)
    smem = pl.BlockSpec(memory_space=pltpu.SMEM)
    rim = jax.ShapeDtypeStruct(before.shape, jnp.float32)
    ext_rows = band + 2 * HALO
    return pl.pallas_call(
        ptycho_kernel,
        out_shape=(rim, jax.ShapeDtypeStruct(own.shape, jnp.float32), rim),
        in_specs=[smem, smem] + [vmem] * 10,
        out_specs=(vmem, vmem, vmem),
        scratch_shapes=[
            pltpu.VMEM((2, NW // PC, ext_rows, PC), jnp.float32),
            pltpu.VMEM((2, NW // PC, ext_rows, PC), jnp.float32),
            pltpu.VMEM((2, PR, PC), jnp.float32),
        ],
        cost_estimate=pl.CostEstimate(
            flops=2000000000, bytes_accessed=2000000, transcendentals=500000
        ),
    )(rows, cols, before, own, after, measured, field, mask, *tables)


MESH = pl.DeviceIdType.MESH


def tail_kernel(
    groups, tiles, capacity,
    wanted_ref, place_ref, slot_ref, used_ref, live_ref,
    top_ref, mid_ref, bottom_ref, proj_ref, mult_ref, prior_ref, weight_ref, vol_ref,
    updated_ref, new_vol_ref, new_mult_ref,
    above_ref, below_ref, moved_ref, mult_moved_ref, half_send_ref,
    send_a, send_b, send_c, recv_a, recv_b, recv_c, spread_ref, wide_ref,
    send_sem, recv_sem, near_send, near_recv,
):
    g = lax.axis_index("angle")
    t = lax.axis_index("tile")
    h = lax.axis_index("half")
    band = proj_ref.shape[2]
    part = band // 2
    places = groups * capacity
    slots = weight_ref.shape[0]
    own_blocks = vol_ref.shape[0]
    has_up = t > 0
    has_down = t < tiles - 1
    half = jnp.bfloat16
    sends = (send_a, send_b, send_c)
    recvs = (recv_a, recv_b, recv_c)

    barrier = pltpu.get_barrier_semaphore()

    def greet(where):
        pl.semaphore_signal(barrier, inc=1, device_id=where, device_id_type=MESH)

    for d in range(1, groups):
        greet({"angle": lax.rem(g + d, groups)})
    greet({"half": 1 - h})

    @pl.when(has_up)
    def _():
        greet({"tile": t - 1})

    @pl.when(has_down)
    def _():
        greet({"tile": t + 1})

    def pick(n, carry):
        send_a[n] = vol_ref[wanted_ref[n]].astype(half)
        return carry

    lax.fori_loop(0, places, pick, 0, unroll=True)
    pl.semaphore_wait(barrier, groups + has_up.astype(jnp.int32) + has_down.astype(jnp.int32))

    def exchange(phase):
        copies = []
        for d in range(1, groups):
            peer = lax.rem(g + d, groups)
            copy = pltpu.make_async_remote_copy(
                src_ref=sends[phase].at[pl.ds(peer * capacity, capacity)],
                dst_ref=recvs[phase].at[pl.ds(g * capacity, capacity)],
                send_sem=send_sem.at[phase, d],
                recv_sem=recv_sem.at[phase, d],
                device_id={"angle": peer},
                device_id_type=MESH,
            )
            copy.start()
            copies.append(copy)
        own = pl.ds(g * capacity, capacity)
        recvs[phase][own] = sends[phase][own]
        return copies

    def near(index, source, target, where):
        return pltpu.make_async_remote_copy(
            src_ref=source,
            dst_ref=target,
            send_sem=near_send.at[index],
            recv_sem=near_recv.at[index],
            device_id=where,
            device_id_type=MESH,
        )

    down_copy = near(0, bottom_ref, above_ref, {"tile": jnp.minimum(t + 1, tiles - 1)})
    up_copy = near(1, top_ref, below_ref, {"tile": jnp.maximum(t - 1, 0)})

    @pl.when(has_down)
    def _():
        down_copy.start()

    @pl.when(has_up)
    def _():
        up_copy.start()

    away = pl.ds(pl.multiple_of((1 - h) * part, part), part)
    here = pl.ds(pl.multiple_of(h * part, part), part)
    mult_copy = near(2, mult_ref.at[0, :, away, :], mult_moved_ref.at[h], {"half": 1 - h})
    mult_copy.start()
    fetches = exchange(0)
    mult_moved_ref[h] = mult_ref[0, :, here, :]

    @pl.when(jnp.logical_not(has_up))
    def _():
        above_ref[...] = jnp.zeros_like(above_ref)

    @pl.when(jnp.logical_not(has_down))
    def _():
        below_ref[...] = jnp.zeros_like(below_ref)

    @pl.when(has_up)
    def _():
        down_copy.wait_recv()

    @pl.when(has_down)
    def _():
        up_copy.wait_recv()

    old = proj_ref[0]
    base = mid_ref[0]
    if band == HALO:
        gradient = base + above_ref[0] + below_ref[0]
    else:
        still = jnp.zeros((2, band - HALO, NW), jnp.float32)
        gradient = base + jnp.concatenate([above_ref[0], still], axis=1)
        gradient = gradient + jnp.concatenate([still, below_ref[0]], axis=1)
    new_re = old[0] - descent * (gradient[0] + penalty * (old[0] - 1.0) + mult_ref[0, 0])
    new_im = old[1] - descent * (gradient[1] + penalty * (old[1] - prior_ref[0]) + mult_ref[0, 1])
    updated_ref[0, 0] = new_re
    updated_ref[0, 1] = new_im
    half_send_ref[...] = updated_ref[0, :, away, :]
    moved_copy = near(3, half_send_ref, moved_ref.at[h], {"half": 1 - h})
    moved_copy.start()
    moved_ref[h] = updated_ref[0, :, here, :]
    for copy in fetches:
        copy.wait_recv()
    mult_copy.wait_recv()

    per_block = CMAX

    def projected(phase, pair):
        total = jnp.zeros((part, RB), jnp.float32)
        for c in range(per_block):
            slot = pair * per_block + c
            picked = recvs[phase][place_ref[slot]]
            total = total + live_ref[slot] * lax.dot_general(
                picked, weight_ref[slot], (((1,), (1,)), ((), ())),
                preferred_element_type=jnp.float32,
            )
        return total

    pairs = slots // per_block
    sinos = [projected(0, pair) for pair in range(pairs)]
    moved_copy.wait_recv()
    for pair in range(pairs):
        angle, k = divmod(pair, NRB)
        rays = slice(k * RB, (k + 1) * RB)
        target = moved_ref[angle, 1, :, rays] + mult_moved_ref[angle, 1, :, rays] / penalty
        residual = (sinos[pair] - target).astype(half)
        for c in range(per_block):
            slot = pair * per_block + c
            spread = live_ref[slot] * jnp.dot(
                residual, weight_ref[slot], preferred_element_type=jnp.float32
            )
            spread_ref[slot] = spread.astype(half)
    for n in range(places):
        send_b[n] = spread_ref[slot_ref[n]] * used_ref[n].astype(half)
    terms = exchange(1)
    for copy in terms:
        copy.wait_recv()
    for n in range(places):
        wide_ref[n] = recv_b[n].astype(jnp.float32)

    def renew(j, carry):
        total = jnp.zeros(wide_ref.shape[1:], jnp.float32)
        for n in range(places):
            total = total + jnp.where(wanted_ref[n] == j, 1.0, 0.0) * wide_ref[n]
        block = vol_ref[j]
        new_vol_ref[j] = block - volume_step * (total + damping * block)
        return carry

    lax.fori_loop(0, own_blocks, renew, 0)
    for n in range(places):
        send_c[n] = new_vol_ref[wanted_ref[n]].astype(half)
    renewals = exchange(2)
    for angle in range(moved_ref.shape[0]):
        new_mult_ref[angle, 0] = mult_moved_ref[angle, 0] + penalty * (moved_ref[angle, 0] - 1.0)
    for copy in renewals:
        copy.wait_recv()
    for pair in range(pairs):
        angle, k = divmod(pair, NRB)
        rays = slice(k * RB, (k + 1) * RB)
        fresh = projected(2, pair)
        new_mult_ref[angle, 1, :, rays] = mult_moved_ref[angle, 1, :, rays] + penalty * (
            moved_ref[angle, 1, :, rays] - fresh
        )
    for copy in fetches + terms + renewals + [mult_copy, moved_copy]:
        copy.wait_send()

    @pl.when(has_down)
    def _():
        down_copy.wait_send()

    @pl.when(has_up)
    def _():
        up_copy.wait_send()


def finish(scalars, arrays, capacity):
    top, mid, bottom, projection, multiplier, prior, weights, volume = arrays
    groups = lax.axis_size("angle")
    tiles = lax.axis_size("tile")
    places = groups * capacity
    slots = weights.shape[0]
    part = projection.shape[2] // 2
    vmem = pl.BlockSpec(memory_space=pltpu.VMEM)
    smem = pl.BlockSpec(memory_space=pltpu.SMEM)
    block = volume.shape[1:]
    moved_shape = (2, 2, part, NW)
    return pl.pallas_call(
        functools.partial(tail_kernel, groups, tiles, capacity),
        out_shape=(
            jax.ShapeDtypeStruct(projection.shape, jnp.float32),
            jax.ShapeDtypeStruct(volume.shape, jnp.float32),
            jax.ShapeDtypeStruct(moved_shape, jnp.float32),
        ),
        in_specs=[smem] * 5 + [vmem] * 8,
        out_specs=(vmem, vmem, vmem),
        scratch_shapes=[
            pltpu.VMEM(bottom.shape, jnp.float32),
            pltpu.VMEM(top.shape, jnp.float32),
            pltpu.VMEM(moved_shape, jnp.float32),
            pltpu.VMEM(moved_shape, jnp.float32),
            pltpu.VMEM(moved_shape[1:], jnp.float32),
            *[pltpu.VMEM((places,) + block, jnp.bfloat16)] * 6,
            pltpu.VMEM((slots,) + block, jnp.bfloat16),
            pltpu.VMEM((places,) + block, jnp.float32),
            pltpu.SemaphoreType.DMA((3, groups)),
            pltpu.SemaphoreType.DMA((3, groups)),
            pltpu.SemaphoreType.DMA((4,)),
            pltpu.SemaphoreType.DMA((4,)),
        ],
        compiler_params=pltpu.CompilerParams(collective_id=1, has_side_effects=True),
    )(*scalars, *arrays)


def shards(
    projection,
    multiplier,
    reprojection,
    intensity,
    row_start,
    column_start,
    probe_field,
    probe_mask,
    weights,
    ray_blocks,
    ray_counts,
    volume,
):
    up, down = neighbours("tile")
    band_rows = projection.shape[2]
    before = lax.ppermute(projection[:, :, band_rows - HALO :], "tile", up)
    after = lax.ppermute(projection[:, :, :HALO], "tile", down)
    top, gradient, bottom = patch_sums(
        before, projection, after, row_start, column_start, intensity, probe_field, probe_mask
    )
    angle_count = weights.shape[0]
    own_blocks = volume.shape[0]
    live = lax.iota(jnp.int32, CMAX)[None, None, :] < ray_counts[:, :, None]
    groups = lax.axis_size("angle")
    slot_count = angle_count * NRB * CMAX
    capacity = max(2, -(-slot_count // groups))
    flat_ids = ray_blocks.reshape(slot_count)
    owners = flat_ids // own_blocks
    local_ids = flat_ids % own_blocks
    owner_hits = (owners[:, None] == lax.iota(jnp.int32, groups)[None, :]).astype(jnp.int32)
    slot_ranks = jnp.sum((jnp.cumsum(owner_hits, axis=0) - 1) * owner_hits, axis=1)
    slot_place = owners * capacity + slot_ranks
    requests = (
        jnp.zeros((groups * capacity,), jnp.int32)
        .at[slot_place]
        .set(local_ids)
        .reshape(groups, capacity)
    )
    wanted = lax.all_to_all(requests, "angle", split_axis=0, concat_axis=0, tiled=True).reshape(
        groups * capacity
    )
    places = lax.iota(jnp.int32, groups * capacity)
    hits = (places[:, None] == slot_place[None, :]).astype(jnp.int32)
    place_slot = jnp.sum(hits * lax.iota(jnp.int32, slot_count)[None, :], axis=1)
    place_used = jnp.sum(hits, axis=1).astype(jnp.float32)
    live_scale = live.reshape(slot_count).astype(jnp.float32)
    scalars = (wanted, slot_place, place_slot, place_used, live_scale)
    tiles = weights.reshape(slot_count, RB, PIX)
    arrays = (top, gradient, bottom, projection, multiplier, reprojection, tiles, volume)
    return finish(scalars, arrays, capacity)


def solution(mesh):
    return jax.shard_map(
        shards,
        mesh=mesh,
        in_specs=(
            P(("angle", "half"), None, "tile", None),
            P(("angle", "half"), None, "tile", None),
            P(("angle", "half"), "tile", None),
            P(("angle", "half"), "tile", None, None),
            P(("angle", "half"), "tile"),
            P(("angle", "half"), "tile"),
            P(),
            P(),
            P("angle", None, None, None, None),
            P("angle", None, None),
            P("angle", None),
            P("angle", ("tile", "half"), None),
        ),
        out_specs=(
            P(("angle", "half"), None, "tile", None),
            P("angle", ("tile", "half"), None),
            P("angle", None, ("tile", "half"), None),
        ),
        check_vma=False,
    )
```

```python
import functools

import jax
import jax.numpy as jnp
import numpy as np
from jax import lax
from jax.experimental import pallas as pl
from jax.experimental.pallas import tpu as pltpu
from jax.sharding import PartitionSpec as P

PR = 64
PC = 128
NW = 256
PIX = 512
RB = 128
CMAX = 4
HALO = 32
NRB = 2


penalty = 0.5
descent = 0.25
volume_step = 1.0
damping = 0.1


def dft_blocks(sign):
    def table(length):
        counter = np.arange(length)
        phase = (counter[:, None] * counter[None, :] % length) * (2.0 * np.pi / length)
        return np.cos(phase) / np.sqrt(length), sign * np.sin(phase) / np.sqrt(length)

    row_cos, row_sin = table(PR)
    col_cos, col_sin = table(PC)
    left = np.block([[row_cos, -row_sin], [row_sin, row_cos]])
    right = np.block([[col_cos, col_sin], [-col_sin, col_cos]])
    return left.astype(np.float32), right.astype(np.float32)


MESH = pl.DeviceIdType.MESH


def head_kernel(groups, tiles, proj_ref, ids_ref, before_ref, after_ref, all_ref, near_send, near_recv, send_sem, recv_sem):
    g = lax.axis_index("angle")
    t = lax.axis_index("tile")
    band = proj_ref.shape[2]
    has_up = t > 0
    has_down = t < tiles - 1
    barrier = pltpu.get_barrier_semaphore()

    def greet(where):
        pl.semaphore_signal(barrier, inc=1, device_id=where, device_id_type=MESH)

    for d in range(1, groups):
        greet({"angle": lax.rem(g + d, groups)})

    @pl.when(has_up)
    def _():
        greet({"tile": t - 1})

    @pl.when(has_down)
    def _():
        greet({"tile": t + 1})

    pl.semaphore_wait(barrier, groups - 1 + has_up.astype(jnp.int32) + has_down.astype(jnp.int32))
    copies = []
    for d in range(1, groups):
        copy = pltpu.make_async_remote_copy(
            src_ref=ids_ref,
            dst_ref=all_ref.at[g],
            send_sem=send_sem.at[d],
            recv_sem=recv_sem.at[d],
            device_id={"angle": lax.rem(g + d, groups)},
            device_id_type=MESH,
        )
        copy.start()
        copies.append(copy)

    def near(index, source, target, where):
        return pltpu.make_async_remote_copy(
            src_ref=source,
            dst_ref=target,
            send_sem=near_send.at[index],
            recv_sem=near_recv.at[index],
            device_id=where,
            device_id_type=MESH,
        )

    last = proj_ref.at[:, :, band - HALO :, :]
    first = proj_ref.at[:, :, :HALO, :]
    down_copy = near(0, last, before_ref, {"tile": jnp.minimum(t + 1, tiles - 1)})
    up_copy = near(1, first, after_ref, {"tile": jnp.maximum(t - 1, 0)})

    @pl.when(has_down)
    def _():
        down_copy.start()

    @pl.when(has_up)
    def _():
        up_copy.start()

    all_ref[g] = ids_ref[...]

    @pl.when(jnp.logical_not(has_up))
    def _():
        before_ref[...] = jnp.zeros_like(before_ref)

    @pl.when(jnp.logical_not(has_down))
    def _():
        after_ref[...] = jnp.zeros_like(after_ref)

    @pl.when(has_up)
    def _():
        down_copy.wait_recv()
        up_copy.wait_send()

    @pl.when(has_down)
    def _():
        up_copy.wait_recv()
        down_copy.wait_send()

    for copy in copies:
        copy.wait()


def gather_head(projection, ray_blocks):
    groups = lax.axis_size("angle")
    tiles = lax.axis_size("tile")
    slots = ray_blocks.size
    vmem = pl.BlockSpec(memory_space=pltpu.VMEM)
    rim = jax.ShapeDtypeStruct(projection.shape[:2] + (HALO, NW), jnp.float32)
    return pl.pallas_call(
        functools.partial(head_kernel, groups, tiles),
        out_shape=(rim, rim, jax.ShapeDtypeStruct((groups, 1, slots), jnp.int32)),
        in_specs=[vmem] * 2,
        out_specs=(vmem, vmem, vmem),
        scratch_shapes=[
            pltpu.SemaphoreType.DMA((2,)),
            pltpu.SemaphoreType.DMA((2,)),
            pltpu.SemaphoreType.DMA((groups,)),
            pltpu.SemaphoreType.DMA((groups,)),
        ],
        compiler_params=pltpu.CompilerParams(collective_id=2, has_side_effects=True),
    )(projection, ray_blocks.reshape(1, slots))


def fill_tables(own_blocks, all_ref, counts_ref, wanted_ref, place_ref, slot_ref, used_ref, live_ref):
    g = lax.axis_index("angle")
    groups, _, slots = all_ref.shape
    capacity = wanted_ref.shape[0] // groups
    mine = [all_ref[g, 0, s] for s in range(slots)]
    owners = [lax.div(b, own_blocks) for b in mine]
    for s in range(slots):
        rank = jnp.int32(0)
        for earlier in range(s):
            rank = rank + jnp.where(owners[earlier] == owners[s], 1, 0)
        place_ref[s] = owners[s] * capacity + rank
        angle, block = divmod(s // CMAX, NRB)
        live_ref[s] = jnp.where(s % CMAX < counts_ref[angle, block], 1.0, 0.0)

    def clear(n, carry):
        wanted_ref[n] = 0
        slot_ref[n] = 0
        used_ref[n] = 0.0
        return carry

    lax.fori_loop(0, groups * capacity, clear, 0)
    for s in range(slots):
        place = place_ref[s]
        slot_ref[place] = s
        used_ref[place] = 1.0

    def group(peer, carry):
        found = jnp.int32(0)
        for s in range(slots):
            b = all_ref[peer, 0, s]
            hit = lax.div(b, own_blocks) == g

            @pl.when(hit)
            def _(found=found, b=b):
                wanted_ref[peer * capacity + found] = lax.rem(b, own_blocks)

            found = found + jnp.where(hit, 1, 0)
        return carry

    lax.fori_loop(0, groups, group, 0)


def write_kernel(a_ref, b_ref, c_ref, a_out, b_out, c_out, sems):
    copies = [
        pltpu.make_async_copy(source, target, sems.at[i])
        for i, (source, target) in enumerate(((a_ref, a_out), (b_ref, b_out), (c_ref, c_out)))
    ]
    for copy in copies:
        copy.start()
    for copy in copies:
        copy.wait()


def write_out(values):
    return pl.pallas_call(
        write_kernel,
        out_shape=tuple(jax.ShapeDtypeStruct(v.shape, v.dtype) for v in values),
        in_specs=[pl.BlockSpec(memory_space=pltpu.VMEM)] * 3,
        out_specs=tuple([pl.BlockSpec(memory_space=pl.ANY)] * 3),
        scratch_shapes=[pltpu.SemaphoreType.DMA((3,))],
    )(*values)


CHUNK = 4


def ptycho_kernel(
    own_blocks, all_ref, counts_ref, rows_ref, cols_ref, before_ref, own_ref, after_ref, measured_ref, field_ref, mask_ref,
    left_f_ref, right_f_ref, left_b_ref, right_b_ref,
    top_ref, mid_ref, bottom_ref, wanted_ref, place_ref, slot_ref, used_ref, live_ref,
    ext_ref, acc_ref, wave_ref,
):
    fill_tables(
        own_blocks, all_ref, counts_ref, wanted_ref, place_ref, slot_ref, used_ref, live_ref
    )
    band = own_ref.shape[2]
    lanes = [slice(0, PC), slice(PC, NW)]
    for side in range(2):
        ext_ref[:, side, :HALO] = before_ref[0, :, :, lanes[side]]
        ext_ref[:, side, HALO : HALO + band] = own_ref[0, :, :, lanes[side]]
        ext_ref[:, side, HALO + band :] = after_ref[0, :, :, lanes[side]]
    acc_ref[...] = jnp.zeros_like(acc_ref)
    half = jnp.bfloat16
    mask = mask_ref[...].astype(jnp.float32)
    wave_ref[0] = field_ref[0] * mask
    wave_ref[1] = field_ref[1] * mask

    lane = lax.broadcasted_iota(jnp.int32, (PR, PC), 1)

    def dot(a, b):
        return jnp.dot(a, b, preferred_element_type=jnp.float32)

    def step(chunk, carry):
        waves = []
        places = []
        for j in range(CHUNK):
            p = chunk * CHUNK + j
            row = rows_ref[0, p] + HALO
            col = cols_ref[0, p]
            places.append((row, col))
            back_shift = lax.rem(NW - col, PC)

            def window(channel):
                near = pltpu.roll(ext_ref[channel, 0, pl.ds(row, PR), :], back_shift, 1)
                next_ = pltpu.roll(ext_ref[channel, 1, pl.ds(row, PR), :], back_shift, 1)
                return jnp.where(lane + col < PC, near, next_)

            o_re = window(0)
            o_im = window(1)
            p_re, p_im = wave_ref[0], wave_ref[1]
            waves.append(
                jnp.concatenate([p_re * o_re - p_im * o_im, p_re * o_im + p_im * o_re], axis=0)
            )
        wide = jnp.concatenate(waves, axis=1).astype(half)
        first = dot(left_f_ref[...], wide).astype(half)
        tall = jnp.concatenate(
            [
                jnp.concatenate(
                    [first[:PR, j * PC : (j + 1) * PC], first[PR:, j * PC : (j + 1) * PC]], axis=1
                )
                for j in range(CHUNK)
            ],
            axis=0,
        )
        far = dot(tall, right_f_ref[...])
        f_re, f_im = far[:, :PC], far[:, PC:]
        measured = measured_ref[0, pl.ds(chunk * CHUNK, CHUNK)].astype(jnp.float32)
        measured = measured.reshape(CHUNK * PR, PC)
        factor = 1.0 - jnp.sqrt(measured) * lax.rsqrt(f_re * f_re + f_im * f_im + 1.0)
        scaled = jnp.concatenate([f_re * factor, f_im * factor], axis=1).astype(half)
        second = dot(scaled, right_b_ref[...]).astype(half)
        wide = jnp.concatenate(
            [
                jnp.concatenate(
                    [second[j * PR : (j + 1) * PR, :PC], second[j * PR : (j + 1) * PR, PC:]], axis=0
                )
                for j in range(CHUNK)
            ],
            axis=1,
        )
        back = dot(left_b_ref[...], wide)
        for j in range(CHUNK):
            row, col = places[j]
            b_re = back[:PR, j * PC : (j + 1) * PC]
            b_im = back[PR:, j * PC : (j + 1) * PC]
            p_re, p_im = wave_ref[0], wave_ref[1]
            shift = lax.rem(col, PC)
            for channel, values in ((0, p_re * b_re + p_im * b_im), (1, p_re * b_im - p_im * b_re)):
                values = pltpu.roll(values, shift, 1)
                acc_ref[channel, 0, pl.ds(row, PR), :] += jnp.where(lane >= col, values, 0.0)
                acc_ref[channel, 1, pl.ds(row, PR), :] += jnp.where(lane >= col, 0.0, values)
        return carry

    lax.fori_loop(0, rows_ref.shape[1] // CHUNK, step, 0)
    for side in range(2):
        top_ref[0, :, :, lanes[side]] = acc_ref[:, side, :HALO]
        mid_ref[0, :, :, lanes[side]] = acc_ref[:, side, HALO : HALO + band]
        bottom_ref[0, :, :, lanes[side]] = acc_ref[:, side, HALO + band :]


def patch_sums(own_blocks, capacity, ids, counts, before, own, after, rows, cols, measured, field, mask):
    band = own.shape[2]
    slots = ids.shape[2]
    places = ids.shape[0] * capacity
    left_f, right_f = dft_blocks(-1.0)
    left_b, right_b = dft_blocks(1.0)
    tables = [jnp.asarray(m, jnp.bfloat16) for m in (left_f, right_f, left_b, right_b)]
    vmem = pl.BlockSpec(memory_space=pltpu.VMEM)
    smem = pl.BlockSpec(memory_space=pltpu.SMEM)
    rim = jax.ShapeDtypeStruct(before.shape, jnp.float32)
    ext_rows = band + 2 * HALO
    return pl.pallas_call(
        functools.partial(ptycho_kernel, own_blocks),
        out_shape=(
            rim, jax.ShapeDtypeStruct(own.shape, jnp.float32), rim,
            jax.ShapeDtypeStruct((places,), jnp.int32),
            jax.ShapeDtypeStruct((slots,), jnp.int32),
            jax.ShapeDtypeStruct((places,), jnp.int32),
            jax.ShapeDtypeStruct((places,), jnp.float32),
            jax.ShapeDtypeStruct((slots,), jnp.float32),
        ),
        in_specs=[smem] * 4 + [vmem] * 10,
        out_specs=(vmem, vmem, vmem) + (smem,) * 5,
        scratch_shapes=[
            pltpu.VMEM((2, NW // PC, ext_rows, PC), jnp.float32),
            pltpu.VMEM((2, NW // PC, ext_rows, PC), jnp.float32),
            pltpu.VMEM((2, PR, PC), jnp.float32),
        ],
        cost_estimate=pl.CostEstimate(
            flops=2000000000, bytes_accessed=2000000, transcendentals=500000
        ),
    )(ids, counts, rows, cols, before, own, after, measured, field, mask, *tables)


def tail_kernel(
    groups, tiles, capacity,
    wanted_ref, place_ref, slot_ref, used_ref, live_ref,
    top_ref, mid_ref, bottom_ref, proj_ref, mult_ref, prior_ref, weight_ref, vol_ref,
    updated_ref, new_vol_ref, new_mult_ref,
    above_ref, below_ref, moved_ref, mult_moved_ref, half_send_ref,
    send_a, send_b, send_c, recv_a, recv_b, recv_c, spread_ref, wide_ref,
    send_sem, recv_sem, near_send, near_recv,
):
    g = lax.axis_index("angle")
    t = lax.axis_index("tile")
    h = lax.axis_index("half")
    band = proj_ref.shape[2]
    part = band // 2
    places = groups * capacity
    slots = weight_ref.shape[0]
    own_blocks = vol_ref.shape[0]
    has_up = t > 0
    has_down = t < tiles - 1
    half = jnp.bfloat16
    sends = (send_a, send_b, send_c)
    recvs = (recv_a, recv_b, recv_c)

    barrier = pltpu.get_barrier_semaphore()

    def greet(where):
        pl.semaphore_signal(barrier, inc=1, device_id=where, device_id_type=MESH)

    for d in range(1, groups):
        greet({"angle": lax.rem(g + d, groups)})
    greet({"half": 1 - h})

    @pl.when(has_up)
    def _():
        greet({"tile": t - 1})

    @pl.when(has_down)
    def _():
        greet({"tile": t + 1})

    def pick(n, carry):
        send_a[n] = vol_ref[wanted_ref[n]].astype(half)
        return carry

    lax.fori_loop(0, places, pick, 0, unroll=True)
    pl.semaphore_wait(barrier, groups + has_up.astype(jnp.int32) + has_down.astype(jnp.int32))

    def exchange(phase):
        copies = []
        for d in range(1, groups):
            peer = lax.rem(g + d, groups)
            copy = pltpu.make_async_remote_copy(
                src_ref=sends[phase].at[pl.ds(peer * capacity, capacity)],
                dst_ref=recvs[phase].at[pl.ds(g * capacity, capacity)],
                send_sem=send_sem.at[phase, d],
                recv_sem=recv_sem.at[phase, d],
                device_id={"angle": peer},
                device_id_type=MESH,
            )
            copy.start()
            copies.append(copy)
        own = pl.ds(g * capacity, capacity)
        recvs[phase][own] = sends[phase][own]
        return copies

    def near(index, source, target, where):
        return pltpu.make_async_remote_copy(
            src_ref=source,
            dst_ref=target,
            send_sem=near_send.at[index],
            recv_sem=near_recv.at[index],
            device_id=where,
            device_id_type=MESH,
        )

    down_copy = near(0, bottom_ref, above_ref, {"tile": jnp.minimum(t + 1, tiles - 1)})
    up_copy = near(1, top_ref, below_ref, {"tile": jnp.maximum(t - 1, 0)})

    @pl.when(has_down)
    def _():
        down_copy.start()

    @pl.when(has_up)
    def _():
        up_copy.start()

    away = pl.ds(pl.multiple_of((1 - h) * part, part), part)
    here = pl.ds(pl.multiple_of(h * part, part), part)
    mult_copy = near(2, mult_ref.at[0, :, away, :], mult_moved_ref.at[h], {"half": 1 - h})
    mult_copy.start()
    fetches = exchange(0)
    mult_moved_ref[h] = mult_ref[0, :, here, :]

    @pl.when(jnp.logical_not(has_up))
    def _():
        above_ref[...] = jnp.zeros_like(above_ref)

    @pl.when(jnp.logical_not(has_down))
    def _():
        below_ref[...] = jnp.zeros_like(below_ref)

    @pl.when(has_up)
    def _():
        down_copy.wait_recv()

    @pl.when(has_down)
    def _():
        up_copy.wait_recv()

    old = proj_ref[0]
    base = mid_ref[0]
    if band == HALO:
        gradient = base + above_ref[0] + below_ref[0]
    else:
        still = jnp.zeros((2, band - HALO, NW), jnp.float32)
        gradient = base + jnp.concatenate([above_ref[0], still], axis=1)
        gradient = gradient + jnp.concatenate([still, below_ref[0]], axis=1)
    new_re = old[0] - descent * (gradient[0] + penalty * (old[0] - 1.0) + mult_ref[0, 0])
    new_im = old[1] - descent * (gradient[1] + penalty * (old[1] - prior_ref[0]) + mult_ref[0, 1])
    updated_ref[0, 0] = new_re
    updated_ref[0, 1] = new_im
    half_send_ref[...] = updated_ref[0, :, away, :]
    moved_copy = near(3, half_send_ref, moved_ref.at[h], {"half": 1 - h})
    moved_copy.start()
    moved_ref[h] = updated_ref[0, :, here, :]
    for copy in fetches:
        copy.wait_recv()
    mult_copy.wait_recv()

    per_block = CMAX

    def projected(phase, pair):
        total = jnp.zeros((part, RB), jnp.float32)
        for c in range(per_block):
            slot = pair * per_block + c
            picked = recvs[phase][place_ref[slot]]
            total = total + live_ref[slot] * lax.dot_general(
                picked, weight_ref[slot], (((1,), (1,)), ((), ())),
                preferred_element_type=jnp.float32,
            )
        return total

    pairs = slots // per_block
    sinos = [projected(0, pair) for pair in range(pairs)]
    moved_copy.wait_recv()
    for pair in range(pairs):
        angle, k = divmod(pair, NRB)
        rays = slice(k * RB, (k + 1) * RB)
        target = moved_ref[angle, 1, :, rays] + mult_moved_ref[angle, 1, :, rays] / penalty
        residual = (sinos[pair] - target).astype(half)
        for c in range(per_block):
            slot = pair * per_block + c
            spread = live_ref[slot] * jnp.dot(
                residual, weight_ref[slot], preferred_element_type=jnp.float32
            )
            spread_ref[slot] = spread.astype(half)
    for n in range(places):
        send_b[n] = spread_ref[slot_ref[n]] * used_ref[n].astype(half)
    terms = exchange(1)
    for copy in terms:
        copy.wait_recv()
    for n in range(places):
        wide_ref[n] = recv_b[n].astype(jnp.float32)

    def renew(j, carry):
        total = jnp.zeros(wide_ref.shape[1:], jnp.float32)
        for n in range(places):
            total = total + jnp.where(wanted_ref[n] == j, 1.0, 0.0) * wide_ref[n]
        block = vol_ref[j]
        new_vol_ref[j] = block - volume_step * (total + damping * block)
        return carry

    lax.fori_loop(0, own_blocks, renew, 0)
    for n in range(places):
        send_c[n] = new_vol_ref[wanted_ref[n]].astype(half)
    renewals = exchange(2)
    for angle in range(moved_ref.shape[0]):
        new_mult_ref[angle, 0] = mult_moved_ref[angle, 0] + penalty * (moved_ref[angle, 0] - 1.0)
    for copy in renewals:
        copy.wait_recv()
    for pair in range(pairs):
        angle, k = divmod(pair, NRB)
        rays = slice(k * RB, (k + 1) * RB)
        fresh = projected(2, pair)
        new_mult_ref[angle, 1, :, rays] = mult_moved_ref[angle, 1, :, rays] + penalty * (
            moved_ref[angle, 1, :, rays] - fresh
        )
    for copy in fetches + terms + renewals + [mult_copy, moved_copy]:
        copy.wait_send()

    @pl.when(has_down)
    def _():
        down_copy.wait_send()

    @pl.when(has_up)
    def _():
        up_copy.wait_send()


def finish(scalars, arrays, capacity):
    top, mid, bottom, projection, multiplier, prior, weights, volume = arrays
    groups = lax.axis_size("angle")
    tiles = lax.axis_size("tile")
    places = groups * capacity
    slots = weights.shape[0]
    part = projection.shape[2] // 2
    vmem = pl.BlockSpec(memory_space=pltpu.VMEM)
    smem = pl.BlockSpec(memory_space=pltpu.SMEM)
    block = volume.shape[1:]
    moved_shape = (2, 2, part, NW)
    return pl.pallas_call(
        functools.partial(tail_kernel, groups, tiles, capacity),
        out_shape=(
            jax.ShapeDtypeStruct(projection.shape, jnp.float32),
            jax.ShapeDtypeStruct(volume.shape, jnp.float32),
            jax.ShapeDtypeStruct(moved_shape, jnp.float32),
        ),
        in_specs=[smem] * 5 + [vmem] * 8,
        out_specs=(vmem, vmem, vmem),
        scratch_shapes=[
            pltpu.VMEM(bottom.shape, jnp.float32),
            pltpu.VMEM(top.shape, jnp.float32),
            pltpu.VMEM(moved_shape, jnp.float32),
            pltpu.VMEM(moved_shape, jnp.float32),
            pltpu.VMEM(moved_shape[1:], jnp.float32),
            *[pltpu.VMEM((places,) + block, jnp.bfloat16)] * 6,
            pltpu.VMEM((slots,) + block, jnp.bfloat16),
            pltpu.VMEM((places,) + block, jnp.float32),
            pltpu.SemaphoreType.DMA((3, groups)),
            pltpu.SemaphoreType.DMA((3, groups)),
            pltpu.SemaphoreType.DMA((4,)),
            pltpu.SemaphoreType.DMA((4,)),
        ],
        compiler_params=pltpu.CompilerParams(collective_id=1, has_side_effects=True),
    )(*scalars, *arrays)


def shards(
    projection,
    multiplier,
    reprojection,
    intensity,
    row_start,
    column_start,
    probe_field,
    probe_mask,
    weights,
    ray_blocks,
    ray_counts,
    volume,
):
    groups = lax.axis_size("angle")
    slot_count = ray_blocks.size
    own_blocks = volume.shape[0]
    capacity = max(2, -(-slot_count // groups))
    before, after, ids = gather_head(projection, ray_blocks)
    top, gradient, bottom, *scalars = patch_sums(
        own_blocks, capacity, ids, ray_counts, before, projection, after, row_start, column_start,
        intensity, probe_field, probe_mask
    )
    tiles = weights.reshape(slot_count, RB, PIX)
    arrays = (top, gradient, bottom, projection, multiplier, reprojection, tiles, volume)
    return write_out(finish(scalars, arrays, capacity))


def solution(mesh):
    return jax.shard_map(
        shards,
        mesh=mesh,
        in_specs=(
            P(("angle", "half"), None, "tile", None),
            P(("angle", "half"), None, "tile", None),
            P(("angle", "half"), "tile", None),
            P(("angle", "half"), "tile", None, None),
            P(("angle", "half"), "tile"),
            P(("angle", "half"), "tile"),
            P(),
            P(),
            P("angle", None, None, None, None),
            P("angle", None, None),
            P("angle", None),
            P("angle", ("tile", "half"), None),
        ),
        out_specs=(
            P(("angle", "half"), None, "tile", None),
            P("angle", ("tile", "half"), None),
            P("angle", None, ("tile", "half"), None),
        ),
        check_vma=False,
    )
```

```python
import functools

import jax
import jax.numpy as jnp
import numpy as np
from jax import lax
from jax.experimental import pallas as pl
from jax.experimental.pallas import tpu as pltpu
from jax.sharding import PartitionSpec as P

PR = 64
PC = 128
NW = 256
PIX = 512
RB = 128
CMAX = 4
HALO = 32
NRB = 2


penalty = 0.5
descent = 0.25
volume_step = 1.0
damping = 0.1


def dft_blocks(sign):
    def table(length):
        counter = np.arange(length)
        phase = (counter[:, None] * counter[None, :] % length) * (2.0 * np.pi / length)
        return np.cos(phase) / np.sqrt(length), sign * np.sin(phase) / np.sqrt(length)

    row_cos, row_sin = table(PR)
    col_cos, col_sin = table(PC)
    left = np.block([[row_cos, -row_sin], [row_sin, row_cos]])
    right = np.block([[col_cos, col_sin], [-col_sin, col_cos]])
    return left.astype(np.float32), right.astype(np.float32)


MESH = pl.DeviceIdType.MESH
CHUNK = 4


def step_kernel(
    groups, tiles, capacity,
    mine_ref, counts_ref, rows_ref, cols_ref,
    ids_ref, proj_ref, mult_ref, prior_ref, measured_ref, field_ref, mask_ref,
    left_f_ref, right_f_ref, left_b_ref, right_b_ref, vol_ref, weight_hbm,
    updated_ref, new_vol_ref, new_mult_ref,
    all_ref, all_smem, wanted_ref, place_ref, slot_ref, used_ref, live_ref,
    weight_ref, before_ref, after_ref, above_ref, below_ref,
    ext_ref, acc_ref, wave_ref, stage_ref,
    moved_ref, mult_moved_ref, half_send_ref,
    send_a, send_b, send_c, recv_a, recv_b, recv_c, spread_ref, wide_ref,
    send_sem, recv_sem, near_send, near_recv, local_sem,
):
    g = lax.axis_index("angle")
    t = lax.axis_index("tile")
    h = lax.axis_index("half")
    band = proj_ref.shape[2]
    part = band // 2
    places = groups * capacity
    own_blocks = vol_ref.shape[0]
    angles, blocks, per_block = mine_ref.shape
    slots = angles * blocks * per_block
    has_up = t > 0
    has_down = t < tiles - 1
    half = jnp.bfloat16
    sends = (send_a, send_b, send_c)
    recvs = (recv_a, recv_b, recv_c)
    lanes = [slice(0, PC), slice(PC, NW)]

    def where_of(slot):
        pair, c = divmod(slot, per_block)
        angle, block = divmod(pair, blocks)
        return angle, block, c

    barrier = pltpu.get_barrier_semaphore()

    def greet(where):
        pl.semaphore_signal(barrier, inc=1, device_id=where, device_id_type=MESH)

    for d in range(1, groups):
        greet({"angle": lax.rem(g + d, groups)})
    greet({"half": 1 - h})

    @pl.when(has_up)
    def _():
        greet({"tile": t - 1})

    @pl.when(has_down)
    def _():
        greet({"tile": t + 1})

    weight_copy = pltpu.make_async_copy(weight_hbm, weight_ref, local_sem.at[0])
    weight_copy.start()

    owners = [lax.div(mine_ref[where_of(s)], own_blocks) for s in range(slots)]
    my_places = []
    for s in range(slots):
        rank = jnp.int32(0)
        for earlier in range(s):
            rank = rank + jnp.where(owners[earlier] == owners[s], 1, 0)
        my_places.append(owners[s] * capacity + rank)
        place_ref[s] = my_places[s]
        angle, block, c = where_of(s)
        live_ref[s] = jnp.where(c < counts_ref[angle, block], 1.0, 0.0)

    def slot_of(n, carry):
        slot = jnp.int32(0)
        used = jnp.float32(0.0)
        for s in range(slots):
            hit = place_ref[s] == n
            slot = jnp.where(hit, s, slot)
            used = jnp.where(hit, 1.0, used)
        slot_ref[n] = slot
        used_ref[n] = used
        return carry

    pl.semaphore_wait(barrier, groups + has_up.astype(jnp.int32) + has_down.astype(jnp.int32))

    def angle_copy(phase, d, source, target):
        return pltpu.make_async_remote_copy(
            src_ref=source,
            dst_ref=target,
            send_sem=send_sem.at[phase, d],
            recv_sem=recv_sem.at[phase, d],
            device_id={"angle": lax.rem(g + d, groups)},
            device_id_type=MESH,
        )

    id_copies = [angle_copy(3, d, ids_ref, all_ref.at[g]) for d in range(1, groups)]
    for copy in id_copies:
        copy.start()

    def exchange(phase):
        copies = []
        for d in range(1, groups):
            peer = lax.rem(g + d, groups)
            copies.append(
                angle_copy(
                    phase, d,
                    sends[phase].at[pl.ds(peer * capacity, capacity)],
                    recvs[phase].at[pl.ds(g * capacity, capacity)],
                )
            )
            copies[-1].start()
        own = pl.ds(g * capacity, capacity)
        recvs[phase][own] = sends[phase][own]
        return copies

    def near(index, source, target, where):
        return pltpu.make_async_remote_copy(
            src_ref=source,
            dst_ref=target,
            send_sem=near_send.at[index],
            recv_sem=near_recv.at[index],
            device_id=where,
            device_id_type=MESH,
        )

    def to_tiles(index, down_source, down_target, up_source, up_target):
        down = near(index, down_source, down_target, {"tile": jnp.minimum(t + 1, tiles - 1)})
        up = near(index + 1, up_source, up_target, {"tile": jnp.maximum(t - 1, 0)})

        @pl.when(has_down)
        def _():
            down.start()

        @pl.when(has_up)
        def _():
            up.start()

        @pl.when(jnp.logical_not(has_up))
        def _():
            down_target[...] = jnp.zeros_like(down_target)

        @pl.when(jnp.logical_not(has_down))
        def _():
            up_target[...] = jnp.zeros_like(up_target)

        return down, up

    def from_tiles(down, up):
        @pl.when(has_up)
        def _():
            down.wait_recv()

        @pl.when(has_down)
        def _():
            up.wait_recv()

    def sent_to_tiles(down, up):
        @pl.when(has_down)
        def _():
            down.wait_send()

        @pl.when(has_up)
        def _():
            up.wait_send()

    halo = to_tiles(
        0, proj_ref.at[0, :, band - HALO :, :], before_ref, proj_ref.at[0, :, :HALO, :], after_ref
    )
    away = pl.ds(pl.multiple_of((1 - h) * part, part), part)
    here = pl.ds(pl.multiple_of(h * part, part), part)
    mult_copy = near(4, mult_ref.at[0, :, away, :], mult_moved_ref.at[h], {"half": 1 - h})
    mult_copy.start()
    mult_moved_ref[h] = mult_ref[0, :, here, :]
    all_ref[g] = ids_ref[...]
    lax.fori_loop(0, places, slot_of, 0)
    for side in range(2):
        ext_ref[:, side, HALO : HALO + band] = proj_ref[0, :, :, lanes[side]]
    acc_ref[...] = jnp.zeros_like(acc_ref)
    stage_ref[...] = jnp.zeros_like(stage_ref)
    mask = mask_ref[...].astype(jnp.float32)
    wave_ref[0] = field_ref[0] * mask
    wave_ref[1] = field_ref[1] * mask

    for copy in id_copies:
        copy.wait_recv()
    id_local = pltpu.make_async_copy(all_ref, all_smem, local_sem.at[1])
    id_local.start()
    id_local.wait()

    def group(peer, carry):
        found = jnp.int32(0)
        values = [jnp.int32(0)] * capacity
        for s in range(slots):
            b = all_smem[(peer,) + where_of(s)]
            hit = lax.div(b, own_blocks) == g
            inside = lax.rem(b, own_blocks)
            values = [
                jnp.where(jnp.logical_and(hit, found == r), inside, values[r])
                for r in range(capacity)
            ]
            found = found + jnp.where(hit, 1, 0)
        for r in range(capacity):
            wanted_ref[peer * capacity + r] = values[r]
        return carry

    lax.fori_loop(0, groups, group, 0)
    for n in range(places):
        send_a[n] = vol_ref[wanted_ref[n]].astype(half)
    fetches = exchange(0)
    from_tiles(*halo)
    for side in range(2):
        ext_ref[:, side, :HALO] = before_ref[:, :, lanes[side]]
        ext_ref[:, side, HALO + band :] = after_ref[:, :, lanes[side]]

    lane = lax.broadcasted_iota(jnp.int32, (PR, PC), 1)
    ext_rows = band + 2 * HALO
    wide_lane = lax.broadcasted_iota(jnp.int32, (ext_rows, PC), 1)

    def dot(a, b):
        return jnp.dot(a, b, preferred_element_type=jnp.float32)

    def step(chunk, carry):
        waves = []
        spots = []
        for j in range(CHUNK):
            p = chunk * CHUNK + j
            row = rows_ref[0, p] + HALO
            col = cols_ref[0, p]
            spots.append((row, col))
            back_shift = lax.rem(NW - col, PC)

            def window(channel):
                near = pltpu.roll(ext_ref[channel, 0, pl.ds(row, PR), :], back_shift, 1)
                next_ = pltpu.roll(ext_ref[channel, 1, pl.ds(row, PR), :], back_shift, 1)
                return jnp.where(lane + col < PC, near, next_)

            o_re = window(0)
            o_im = window(1)
            p_re, p_im = wave_ref[0], wave_ref[1]
            waves.append(
                jnp.concatenate([p_re * o_re - p_im * o_im, p_re * o_im + p_im * o_re], axis=0)
            )
        wide = jnp.concatenate(waves, axis=1).astype(half)
        first = dot(left_f_ref[...], wide).astype(half)
        tall = jnp.concatenate(
            [
                jnp.concatenate(
                    [first[:PR, j * PC : (j + 1) * PC], first[PR:, j * PC : (j + 1) * PC]], axis=1
                )
                for j in range(CHUNK)
            ],
            axis=0,
        )
        far = dot(tall, right_f_ref[...])
        f_re, f_im = far[:, :PC], far[:, PC:]
        measured = measured_ref[0, pl.ds(chunk * CHUNK, CHUNK)].astype(jnp.float32)
        measured = measured.reshape(CHUNK * PR, PC)
        factor = 1.0 - jnp.sqrt(measured) * lax.rsqrt(f_re * f_re + f_im * f_im + 1.0)
        scaled = jnp.concatenate([f_re * factor, f_im * factor], axis=1).astype(half)
        second = dot(scaled, right_b_ref[...]).astype(half)
        wide = jnp.concatenate(
            [
                jnp.concatenate(
                    [second[j * PR : (j + 1) * PR, :PC], second[j * PR : (j + 1) * PR, PC:]], axis=0
                )
                for j in range(CHUNK)
            ],
            axis=1,
        )
        back = dot(left_b_ref[...], wide)
        above = ext_rows - PR
        for j in range(CHUNK):
            shift = lax.rem(spots[j][1], PC)
            b_re = back[:PR, j * PC : (j + 1) * PC]
            b_im = back[PR:, j * PC : (j + 1) * PC]
            p_re, p_im = wave_ref[0], wave_ref[1]
            stage_ref[j, 0, above : above + PR] = pltpu.roll(p_re * b_re + p_im * b_im, shift, 1)
            stage_ref[j, 1, above : above + PR] = pltpu.roll(p_re * b_im - p_im * b_re, shift, 1)
        for channel in range(2):
            first_half = acc_ref[channel, 0]
            next_half = acc_ref[channel, 1]
            for j in range(CHUNK):
                row, col = spots[j]
                values = stage_ref[j, channel, pl.ds(above - row, ext_rows), :]
                first_half = first_half + jnp.where(wide_lane >= col, values, 0.0)
                next_half = next_half + jnp.where(wide_lane >= col, 0.0, values)
            acc_ref[channel, 0] = first_half
            acc_ref[channel, 1] = next_half
        return carry

    lax.fori_loop(0, rows_ref.shape[1] // CHUNK, step, 0)
    rims = to_tiles(
        2, acc_ref.at[:, :, HALO + band :, :], above_ref, acc_ref.at[:, :, :HALO, :], below_ref
    )
    from_tiles(*rims)
    for side in range(2):
        for channel in range(2):
            gradient = acc_ref[channel, side, HALO : HALO + band]
            above = above_ref[channel, side]
            below = below_ref[channel, side]
            if band == HALO:
                gradient = gradient + above + below
            else:
                still = jnp.zeros((band - HALO, PC), jnp.float32)
                gradient = gradient + jnp.concatenate([above, still], axis=0)
                gradient = gradient + jnp.concatenate([still, below], axis=0)
            old = proj_ref[0, channel, :, lanes[side]]
            held = 1.0 if channel == 0 else prior_ref[0, :, lanes[side]]
            updated_ref[0, channel, :, lanes[side]] = old - descent * (
                gradient + penalty * (old - held) + mult_ref[0, channel, :, lanes[side]]
            )
    half_send_ref[...] = updated_ref[0, :, away, :]
    moved_copy = near(5, half_send_ref, moved_ref.at[h], {"half": 1 - h})
    moved_copy.start()
    moved_ref[h] = updated_ref[0, :, here, :]
    for copy in fetches:
        copy.wait_recv()
    mult_copy.wait_recv()
    weight_copy.wait()

    def projected(phase, pair):
        total = jnp.zeros((part, RB), jnp.float32)
        for c in range(per_block):
            slot = pair * per_block + c
            picked = recvs[phase][place_ref[slot]]
            total = total + live_ref[slot] * lax.dot_general(
                picked, weight_ref[where_of(slot)], (((1,), (1,)), ((), ())),
                preferred_element_type=jnp.float32,
            )
        return total

    pairs = slots // per_block
    sinos = [projected(0, pair) for pair in range(pairs)]
    moved_copy.wait_recv()
    for pair in range(pairs):
        angle, k = divmod(pair, NRB)
        rays = slice(k * RB, (k + 1) * RB)
        target = moved_ref[angle, 1, :, rays] + mult_moved_ref[angle, 1, :, rays] / penalty
        residual = (sinos[pair] - target).astype(half)
        for c in range(per_block):
            slot = pair * per_block + c
            spread = live_ref[slot] * jnp.dot(
                residual, weight_ref[where_of(slot)], preferred_element_type=jnp.float32
            )
            spread_ref[slot] = spread.astype(half)
    for n in range(places):
        send_b[n] = spread_ref[slot_ref[n]] * used_ref[n].astype(half)
    terms = exchange(1)
    for copy in terms:
        copy.wait_recv()
    for n in range(places):
        wide_ref[n] = recv_b[n].astype(jnp.float32)

    def renew(j, carry):
        total = jnp.zeros(wide_ref.shape[1:], jnp.float32)
        for n in range(places):
            total = total + jnp.where(wanted_ref[n] == j, 1.0, 0.0) * wide_ref[n]
        block = vol_ref[j]
        new_vol_ref[j] = block - volume_step * (total + damping * block)
        return carry

    lax.fori_loop(0, own_blocks, renew, 0)
    for n in range(places):
        send_c[n] = new_vol_ref[wanted_ref[n]].astype(half)
    renewals = exchange(2)
    for angle in range(moved_ref.shape[0]):
        new_mult_ref[angle, 0] = mult_moved_ref[angle, 0] + penalty * (moved_ref[angle, 0] - 1.0)
    for copy in renewals:
        copy.wait_recv()
    for pair in range(pairs):
        angle, k = divmod(pair, NRB)
        rays = slice(k * RB, (k + 1) * RB)
        fresh = projected(2, pair)
        new_mult_ref[angle, 1, :, rays] = mult_moved_ref[angle, 1, :, rays] + penalty * (
            moved_ref[angle, 1, :, rays] - fresh
        )
    for copy in id_copies + fetches + terms + renewals + [mult_copy, moved_copy]:
        copy.wait_send()
    sent_to_tiles(*halo)
    sent_to_tiles(*rims)


def admm_step(ray_blocks, counts, rows, cols, own, multiplier, prior, measured, field, mask, volume, weights):
    groups = lax.axis_size("angle")
    tiles = lax.axis_size("tile")
    slots = ray_blocks.size
    capacity = max(2, -(-slots // groups))
    places = groups * capacity
    left_f, right_f = dft_blocks(-1.0)
    left_b, right_b = dft_blocks(1.0)
    tables = [jnp.asarray(m, jnp.bfloat16) for m in (left_f, right_f, left_b, right_b)]
    vmem = pl.BlockSpec(memory_space=pltpu.VMEM)
    smem = pl.BlockSpec(memory_space=pltpu.SMEM)
    band = own.shape[2]
    ext_rows = band + 2 * HALO
    block = volume.shape[1:]
    moved_shape = (2, 2, band // 2, NW)
    ids = (groups,) + ray_blocks.shape
    f32 = jnp.float32
    return pl.pallas_call(
        functools.partial(step_kernel, groups, tiles, capacity),
        out_shape=(
            jax.ShapeDtypeStruct(own.shape, f32),
            jax.ShapeDtypeStruct(volume.shape, f32),
            jax.ShapeDtypeStruct(moved_shape, f32),
        ),
        in_specs=[smem] * 4 + [vmem] * 12 + [pl.BlockSpec(memory_space=pl.ANY)],
        out_specs=(vmem, vmem, vmem),
        scratch_shapes=[
            pltpu.VMEM(ids, jnp.int32),
            pltpu.SMEM(ids, jnp.int32),
            pltpu.SMEM((places,), jnp.int32),
            pltpu.SMEM((slots,), jnp.int32),
            pltpu.SMEM((places,), jnp.int32),
            pltpu.SMEM((places,), f32),
            pltpu.SMEM((slots,), f32),
            pltpu.VMEM(weights.shape, jnp.bfloat16),
            pltpu.VMEM((2, HALO, NW), f32),
            pltpu.VMEM((2, HALO, NW), f32),
            pltpu.VMEM((2, NW // PC, HALO, PC), f32),
            pltpu.VMEM((2, NW // PC, HALO, PC), f32),
            pltpu.VMEM((2, NW // PC, ext_rows, PC), f32),
            pltpu.VMEM((2, NW // PC, ext_rows, PC), f32),
            pltpu.VMEM((2, PR, PC), f32),
            pltpu.VMEM((CHUNK, 2, 2 * (ext_rows - PR) + PR, PC), f32),
            pltpu.VMEM(moved_shape, f32),
            pltpu.VMEM(moved_shape, f32),
            pltpu.VMEM(moved_shape[1:], f32),
            *[pltpu.VMEM((places,) + block, jnp.bfloat16)] * 6,
            pltpu.VMEM((slots,) + block, jnp.bfloat16),
            pltpu.VMEM((places,) + block, f32),
            pltpu.SemaphoreType.DMA((4, groups)),
            pltpu.SemaphoreType.DMA((4, groups)),
            pltpu.SemaphoreType.DMA((6,)),
            pltpu.SemaphoreType.DMA((6,)),
            pltpu.SemaphoreType.DMA((2,)),
        ],
        compiler_params=pltpu.CompilerParams(collective_id=1, has_side_effects=True),
    )(
        ray_blocks, counts, rows, cols,
        ray_blocks, own, multiplier, prior, measured, field, mask, *tables, volume, weights,
    )


def write_kernel(a_ref, b_ref, c_ref, a_out, b_out, c_out, sems):
    copies = [
        pltpu.make_async_copy(source, target, sems.at[i])
        for i, (source, target) in enumerate(((a_ref, a_out), (b_ref, b_out), (c_ref, c_out)))
    ]
    for copy in copies:
        copy.start()
    for copy in copies:
        copy.wait()


def write_out(values):
    return pl.pallas_call(
        write_kernel,
        out_shape=tuple(jax.ShapeDtypeStruct(v.shape, v.dtype) for v in values),
        in_specs=[pl.BlockSpec(memory_space=pltpu.VMEM)] * 3,
        out_specs=tuple([pl.BlockSpec(memory_space=pl.ANY)] * 3),
        scratch_shapes=[pltpu.SemaphoreType.DMA((3,))],
    )(*values)


def shards(
    projection,
    multiplier,
    reprojection,
    intensity,
    row_start,
    column_start,
    probe_field,
    probe_mask,
    weights,
    ray_blocks,
    ray_counts,
    volume,
):
    return write_out(
        admm_step(
            ray_blocks, ray_counts, row_start, column_start, projection, multiplier, reprojection,
            intensity, probe_field, probe_mask, volume, weights,
        )
    )


def solution(mesh):
    return jax.shard_map(
        shards,
        mesh=mesh,
        in_specs=(
            P(("angle", "half"), None, "tile", None),
            P(("angle", "half"), None, "tile", None),
            P(("angle", "half"), "tile", None),
            P(("angle", "half"), "tile", None, None),
            P(("angle", "half"), "tile"),
            P(("angle", "half"), "tile"),
            P(),
            P(),
            P("angle", None, None, None, None),
            P("angle", None, None),
            P("angle", None),
            P("angle", ("tile", "half"), None),
        ),
        out_specs=(
            P(("angle", "half"), None, "tile", None),
            P("angle", ("tile", "half"), None),
            P("angle", None, ("tile", "half"), None),
        ),
        check_vma=False,
    )
```

```python
import functools

import jax
import jax.numpy as jnp
import numpy as np
from jax import lax
from jax.experimental import pallas as pl
from jax.experimental.pallas import tpu as pltpu
from jax.sharding import PartitionSpec as P

PR = 64
PC = 128
NW = 256
PIX = 512
RB = 128
CMAX = 4
HALO = 32
NRB = 2


penalty = 0.5
descent = 0.25
volume_step = 1.0
damping = 0.1


def dft_blocks(sign):
    def table(length):
        counter = np.arange(length)
        phase = (counter[:, None] * counter[None, :] % length) * (2.0 * np.pi / length)
        return np.cos(phase) / np.sqrt(length), sign * np.sin(phase) / np.sqrt(length)

    row_cos, row_sin = table(PR)
    col_cos, col_sin = table(PC)
    left = np.block([[row_cos, -row_sin], [row_sin, row_cos]])
    right = np.block([[col_cos, col_sin], [-col_sin, col_cos]])
    return left.astype(np.float32), right.astype(np.float32)


def split_table(matrix):
    coarse = matrix.astype(jnp.bfloat16)
    rest = (matrix - coarse.astype(np.float32)).astype(jnp.bfloat16)
    return jnp.asarray(np.concatenate([coarse, rest], axis=1))


MESH = pl.DeviceIdType.MESH
CHUNK = 16


def step_kernel(
    groups, tiles, capacity,
    mine_ref, counts_ref, rows_ref, cols_ref,
    ids_ref, proj_ref, mult_ref, prior_ref, measured_ref, field_ref, mask_ref,
    left_f_ref, right_f_ref, left_b_ref, right_b_ref, vol_ref, weight_hbm,
    updated_ref, new_vol_ref, new_mult_ref,
    all_ref, all_smem, wanted_ref, place_ref, slot_ref, used_ref, live_ref,
    weight_ref, before_ref, after_ref, above_ref, below_ref,
    ext_ref, acc_ref, wave_ref, stage_ref,
    moved_ref, mult_moved_ref, half_send_ref,
    send_a, send_b, send_c, recv_a, recv_b, recv_c, spread_ref, wide_ref,
    send_sem, recv_sem, near_send, near_recv, local_sem,
):
    g = lax.axis_index("angle")
    t = lax.axis_index("tile")
    h = lax.axis_index("half")
    band = proj_ref.shape[2]
    part = band // 2
    places = groups * capacity
    own_blocks = vol_ref.shape[0]
    angles, blocks, per_block = mine_ref.shape
    slots = angles * blocks * per_block
    has_up = t > 0
    has_down = t < tiles - 1
    half = jnp.bfloat16
    sends = (send_a, send_b, send_c)
    recvs = (recv_a, recv_b, recv_c)
    lanes = [slice(0, PC), slice(PC, NW)]

    def where_of(slot):
        pair, c = divmod(slot, per_block)
        angle, block = divmod(pair, blocks)
        return angle, block, c

    barrier = pltpu.get_barrier_semaphore()

    def greet(where):
        pl.semaphore_signal(barrier, inc=1, device_id=where, device_id_type=MESH)

    for d in range(1, groups):
        greet({"angle": lax.rem(g + d, groups)})
    greet({"half": 1 - h})

    @pl.when(has_up)
    def _():
        greet({"tile": t - 1})

    @pl.when(has_down)
    def _():
        greet({"tile": t + 1})

    weight_copy = pltpu.make_async_copy(weight_hbm, weight_ref, local_sem.at[0])
    weight_copy.start()

    owners = [lax.div(mine_ref[where_of(s)], own_blocks) for s in range(slots)]
    my_places = []
    for s in range(slots):
        rank = jnp.int32(0)
        for earlier in range(s):
            rank = rank + jnp.where(owners[earlier] == owners[s], 1, 0)
        my_places.append(owners[s] * capacity + rank)
        place_ref[s] = my_places[s]
        angle, block, c = where_of(s)
        live_ref[s] = jnp.where(c < counts_ref[angle, block], 1.0, 0.0)

    def slot_of(n, carry):
        slot = jnp.int32(0)
        used = jnp.float32(0.0)
        for s in range(slots):
            hit = place_ref[s] == n
            slot = jnp.where(hit, s, slot)
            used = jnp.where(hit, 1.0, used)
        slot_ref[n] = slot
        used_ref[n] = used
        return carry

    pl.semaphore_wait(barrier, groups + has_up.astype(jnp.int32) + has_down.astype(jnp.int32))

    def angle_copy(phase, d, source, target):
        return pltpu.make_async_remote_copy(
            src_ref=source,
            dst_ref=target,
            send_sem=send_sem.at[phase, d],
            recv_sem=recv_sem.at[phase, d],
            device_id={"angle": lax.rem(g + d, groups)},
            device_id_type=MESH,
        )

    id_copies = [angle_copy(3, d, ids_ref, all_ref.at[g]) for d in range(1, groups)]
    for copy in id_copies:
        copy.start()

    def exchange(phase):
        copies = []
        for d in range(1, groups):
            peer = lax.rem(g + d, groups)
            copies.append(
                angle_copy(
                    phase, d,
                    sends[phase].at[pl.ds(peer * capacity, capacity)],
                    recvs[phase].at[pl.ds(g * capacity, capacity)],
                )
            )
            copies[-1].start()
        own = pl.ds(g * capacity, capacity)
        recvs[phase][own] = sends[phase][own]
        return copies

    def near(index, source, target, where):
        return pltpu.make_async_remote_copy(
            src_ref=source,
            dst_ref=target,
            send_sem=near_send.at[index],
            recv_sem=near_recv.at[index],
            device_id=where,
            device_id_type=MESH,
        )

    def to_tiles(index, down_source, down_target, up_source, up_target):
        down = near(index, down_source, down_target, {"tile": jnp.minimum(t + 1, tiles - 1)})
        up = near(index + 1, up_source, up_target, {"tile": jnp.maximum(t - 1, 0)})

        @pl.when(has_down)
        def _():
            down.start()

        @pl.when(has_up)
        def _():
            up.start()

        @pl.when(jnp.logical_not(has_up))
        def _():
            down_target[...] = jnp.zeros_like(down_target)

        @pl.when(jnp.logical_not(has_down))
        def _():
            up_target[...] = jnp.zeros_like(up_target)

        return down, up

    def from_tiles(down, up):
        @pl.when(has_up)
        def _():
            down.wait_recv()

        @pl.when(has_down)
        def _():
            up.wait_recv()

    def sent_to_tiles(down, up):
        @pl.when(has_down)
        def _():
            down.wait_send()

        @pl.when(has_up)
        def _():
            up.wait_send()

    halo = to_tiles(
        0, proj_ref.at[0, :, band - HALO :, :], before_ref, proj_ref.at[0, :, :HALO, :], after_ref
    )
    away = pl.ds(pl.multiple_of((1 - h) * part, part), part)
    here = pl.ds(pl.multiple_of(h * part, part), part)
    mult_copy = near(4, mult_ref.at[0, :, away, :], mult_moved_ref.at[h], {"half": 1 - h})
    mult_copy.start()
    mult_moved_ref[h] = mult_ref[0, :, here, :]
    all_ref[g] = ids_ref[...]
    lax.fori_loop(0, places, slot_of, 0)
    for side in range(2):
        ext_ref[:, side, HALO : HALO + band] = proj_ref[0, :, :, lanes[side]]
    acc_ref[...] = jnp.zeros_like(acc_ref)
    stage_ref[...] = jnp.zeros_like(stage_ref)
    mask = mask_ref[...].astype(jnp.float32)
    wave_ref[0] = field_ref[0] * mask
    wave_ref[1] = field_ref[1] * mask

    for copy in id_copies:
        copy.wait_recv()
    id_local = pltpu.make_async_copy(all_ref, all_smem, local_sem.at[1])
    id_local.start()
    id_local.wait()

    def group(peer, carry):
        found = jnp.int32(0)
        values = [jnp.int32(0)] * capacity
        for s in range(slots):
            b = all_smem[(peer,) + where_of(s)]
            hit = lax.div(b, own_blocks) == g
            inside = lax.rem(b, own_blocks)
            values = [
                jnp.where(jnp.logical_and(hit, found == r), inside, values[r])
                for r in range(capacity)
            ]
            found = found + jnp.where(hit, 1, 0)
        for r in range(capacity):
            wanted_ref[peer * capacity + r] = values[r]
        return carry

    lax.fori_loop(0, groups, group, 0)
    for n in range(places):
        send_a[n] = vol_ref[wanted_ref[n]].astype(half)
    fetches = exchange(0)
    from_tiles(*halo)
    for side in range(2):
        ext_ref[:, side, :HALO] = before_ref[:, :, lanes[side]]
        ext_ref[:, side, HALO + band :] = after_ref[:, :, lanes[side]]

    lane = lax.broadcasted_iota(jnp.int32, (PR, PC), 1)
    ext_rows = band + 2 * HALO
    wide_lane = lax.broadcasted_iota(jnp.int32, (ext_rows, PC), 1)

    def dot(a, b):
        return jnp.dot(a, b, preferred_element_type=jnp.float32)

    def step(chunk, carry):
        waves = []
        spots = []
        for j in range(CHUNK):
            p = chunk * CHUNK + j
            row = rows_ref[0, p] + HALO
            col = cols_ref[0, p]
            spots.append((row, col))
            back_shift = lax.rem(NW - col, PC)

            def window(channel):
                near = pltpu.roll(ext_ref[channel, 0, pl.ds(row, PR), :], back_shift, 1)
                next_ = pltpu.roll(ext_ref[channel, 1, pl.ds(row, PR), :], back_shift, 1)
                return jnp.where(lane + col < PC, near, next_)

            o_re = window(0)
            o_im = window(1)
            p_re, p_im = wave_ref[0], wave_ref[1]
            waves.append(
                jnp.concatenate([p_re * o_re - p_im * o_im, p_re * o_im + p_im * o_re], axis=0)
            )
        wide = jnp.concatenate(waves, axis=1).astype(half)
        first = dot(left_f_ref[...], jnp.concatenate([wide, wide], axis=0)).astype(half)
        tall = jnp.concatenate(
            [
                jnp.concatenate(
                    [first[:PR, j * PC : (j + 1) * PC], first[PR:, j * PC : (j + 1) * PC]], axis=1
                )
                for j in range(CHUNK)
            ],
            axis=0,
        )
        far = dot(tall, right_f_ref[...])
        f_re, f_im = far[:, :PC], far[:, PC:]
        measured = measured_ref[0, pl.ds(chunk * CHUNK, CHUNK)].astype(jnp.float32)
        measured = measured.reshape(CHUNK * PR, PC)
        factor = 1.0 - jnp.sqrt(measured) * lax.rsqrt(f_re * f_re + f_im * f_im + 1.0)
        scaled = jnp.concatenate([f_re * factor, f_im * factor], axis=1).astype(half)
        second = dot(scaled, right_b_ref[...]).astype(half)
        wide = jnp.concatenate(
            [
                jnp.concatenate(
                    [second[j * PR : (j + 1) * PR, :PC], second[j * PR : (j + 1) * PR, PC:]], axis=0
                )
                for j in range(CHUNK)
            ],
            axis=1,
        )
        back = dot(left_b_ref[...], jnp.concatenate([wide, wide], axis=0))
        above = ext_rows - PR
        for j in range(CHUNK):
            shift = lax.rem(spots[j][1], PC)
            b_re = back[:PR, j * PC : (j + 1) * PC]
            b_im = back[PR:, j * PC : (j + 1) * PC]
            p_re, p_im = wave_ref[0], wave_ref[1]
            stage_ref[j, 0, above : above + PR] = pltpu.roll(p_re * b_re + p_im * b_im, shift, 1)
            stage_ref[j, 1, above : above + PR] = pltpu.roll(p_re * b_im - p_im * b_re, shift, 1)
        for channel in range(2):
            first_half = acc_ref[channel, 0]
            next_half = acc_ref[channel, 1]
            for j in range(CHUNK):
                row, col = spots[j]
                values = stage_ref[j, channel, pl.ds(above - row, ext_rows), :]
                first_half = first_half + jnp.where(wide_lane >= col, values, 0.0)
                next_half = next_half + jnp.where(wide_lane >= col, 0.0, values)
            acc_ref[channel, 0] = first_half
            acc_ref[channel, 1] = next_half
        return carry

    lax.fori_loop(0, rows_ref.shape[1] // CHUNK, step, 0)
    rims = to_tiles(
        2, acc_ref.at[:, :, HALO + band :, :], above_ref, acc_ref.at[:, :, :HALO, :], below_ref
    )
    from_tiles(*rims)
    for side in range(2):
        for channel in range(2):
            gradient = acc_ref[channel, side, HALO : HALO + band]
            above = above_ref[channel, side]
            below = below_ref[channel, side]
            if band == HALO:
                gradient = gradient + above + below
            else:
                still = jnp.zeros((band - HALO, PC), jnp.float32)
                gradient = gradient + jnp.concatenate([above, still], axis=0)
                gradient = gradient + jnp.concatenate([still, below], axis=0)
            old = proj_ref[0, channel, :, lanes[side]]
            held = 1.0 if channel == 0 else prior_ref[0, :, lanes[side]]
            updated_ref[0, channel, :, lanes[side]] = old - descent * (
                gradient + penalty * (old - held) + mult_ref[0, channel, :, lanes[side]]
            )
    half_send_ref[...] = updated_ref[0, :, away, :]
    moved_copy = near(5, half_send_ref, moved_ref.at[h], {"half": 1 - h})
    moved_copy.start()
    moved_ref[h] = updated_ref[0, :, here, :]
    for copy in fetches:
        copy.wait_recv()
    mult_copy.wait_recv()
    weight_copy.wait()

    def projected(phase, pair):
        total = jnp.zeros((part, RB), jnp.float32)
        for c in range(per_block):
            slot = pair * per_block + c
            picked = recvs[phase][place_ref[slot]]
            total = total + live_ref[slot] * lax.dot_general(
                picked, weight_ref[where_of(slot)], (((1,), (1,)), ((), ())),
                preferred_element_type=jnp.float32,
            )
        return total

    pairs = slots // per_block
    sinos = [projected(0, pair) for pair in range(pairs)]
    moved_copy.wait_recv()
    for pair in range(pairs):
        angle, k = divmod(pair, NRB)
        rays = slice(k * RB, (k + 1) * RB)
        target = moved_ref[angle, 1, :, rays] + mult_moved_ref[angle, 1, :, rays] / penalty
        residual = (sinos[pair] - target).astype(half)
        for c in range(per_block):
            slot = pair * per_block + c
            spread = live_ref[slot] * jnp.dot(
                residual, weight_ref[where_of(slot)], preferred_element_type=jnp.float32
            )
            spread_ref[slot] = spread.astype(half)
    for n in range(places):
        send_b[n] = spread_ref[slot_ref[n]] * used_ref[n].astype(half)
    terms = exchange(1)
    for copy in terms:
        copy.wait_recv()
    for n in range(places):
        wide_ref[n] = recv_b[n].astype(jnp.float32)

    def renew(j, carry):
        total = jnp.zeros(wide_ref.shape[1:], jnp.float32)
        for n in range(places):
            total = total + jnp.where(wanted_ref[n] == j, 1.0, 0.0) * wide_ref[n]
        block = vol_ref[j]
        new_vol_ref[j] = block - volume_step * (total + damping * block)
        return carry

    lax.fori_loop(0, own_blocks, renew, 0)
    for n in range(places):
        send_c[n] = new_vol_ref[wanted_ref[n]].astype(half)
    renewals = exchange(2)
    for angle in range(moved_ref.shape[0]):
        new_mult_ref[angle, 0] = mult_moved_ref[angle, 0] + penalty * (moved_ref[angle, 0] - 1.0)
    for copy in renewals:
        copy.wait_recv()
    for pair in range(pairs):
        angle, k = divmod(pair, NRB)
        rays = slice(k * RB, (k + 1) * RB)
        fresh = projected(2, pair)
        new_mult_ref[angle, 1, :, rays] = mult_moved_ref[angle, 1, :, rays] + penalty * (
            moved_ref[angle, 1, :, rays] - fresh
        )
    for copy in id_copies + fetches + terms + renewals + [mult_copy, moved_copy]:
        copy.wait_send()
    sent_to_tiles(*halo)
    sent_to_tiles(*rims)


def admm_step(ray_blocks, counts, rows, cols, own, multiplier, prior, measured, field, mask, volume, weights):
    groups = lax.axis_size("angle")
    tiles = lax.axis_size("tile")
    slots = ray_blocks.size
    capacity = max(2, -(-slots // groups))
    places = groups * capacity
    left_f, right_f = dft_blocks(-1.0)
    left_b, right_b = dft_blocks(1.0)
    left_f, left_b = (split_table(m) for m in (left_f, left_b))
    tables = [left_f, jnp.asarray(right_f, jnp.bfloat16), left_b, jnp.asarray(right_b, jnp.bfloat16)]
    vmem = pl.BlockSpec(memory_space=pltpu.VMEM)
    smem = pl.BlockSpec(memory_space=pltpu.SMEM)
    band = own.shape[2]
    ext_rows = band + 2 * HALO
    block = volume.shape[1:]
    moved_shape = (2, 2, band // 2, NW)
    ids = (groups,) + ray_blocks.shape
    f32 = jnp.float32
    return pl.pallas_call(
        functools.partial(step_kernel, groups, tiles, capacity),
        out_shape=(
            jax.ShapeDtypeStruct(own.shape, f32),
            jax.ShapeDtypeStruct(volume.shape, f32),
            jax.ShapeDtypeStruct(moved_shape, f32),
        ),
        in_specs=[smem] * 4 + [vmem] * 12 + [pl.BlockSpec(memory_space=pl.ANY)],
        out_specs=(vmem, vmem, vmem),
        scratch_shapes=[
            pltpu.VMEM(ids, jnp.int32),
            pltpu.SMEM(ids, jnp.int32),
            pltpu.SMEM((places,), jnp.int32),
            pltpu.SMEM((slots,), jnp.int32),
            pltpu.SMEM((places,), jnp.int32),
            pltpu.SMEM((places,), f32),
            pltpu.SMEM((slots,), f32),
            pltpu.VMEM(weights.shape, jnp.bfloat16),
            pltpu.VMEM((2, HALO, NW), f32),
            pltpu.VMEM((2, HALO, NW), f32),
            pltpu.VMEM((2, NW // PC, HALO, PC), f32),
            pltpu.VMEM((2, NW // PC, HALO, PC), f32),
            pltpu.VMEM((2, NW // PC, ext_rows, PC), f32),
            pltpu.VMEM((2, NW // PC, ext_rows, PC), f32),
            pltpu.VMEM((2, PR, PC), f32),
            pltpu.VMEM((CHUNK, 2, 2 * (ext_rows - PR) + PR, PC), f32),
            pltpu.VMEM(moved_shape, f32),
            pltpu.VMEM(moved_shape, f32),
            pltpu.VMEM(moved_shape[1:], f32),
            *[pltpu.VMEM((places,) + block, jnp.bfloat16)] * 6,
            pltpu.VMEM((slots,) + block, jnp.bfloat16),
            pltpu.VMEM((places,) + block, f32),
            pltpu.SemaphoreType.DMA((4, groups)),
            pltpu.SemaphoreType.DMA((4, groups)),
            pltpu.SemaphoreType.DMA((6,)),
            pltpu.SemaphoreType.DMA((6,)),
            pltpu.SemaphoreType.DMA((2,)),
        ],
        compiler_params=pltpu.CompilerParams(collective_id=1, has_side_effects=True),
    )(
        ray_blocks, counts, rows, cols,
        ray_blocks, own, multiplier, prior, measured, field, mask, *tables, volume, weights,
    )


def write_kernel(a_ref, b_ref, c_ref, a_out, b_out, c_out, sems):
    copies = [
        pltpu.make_async_copy(source, target, sems.at[i])
        for i, (source, target) in enumerate(((a_ref, a_out), (b_ref, b_out), (c_ref, c_out)))
    ]
    for copy in copies:
        copy.start()
    for copy in copies:
        copy.wait()


def write_out(values):
    return pl.pallas_call(
        write_kernel,
        out_shape=tuple(jax.ShapeDtypeStruct(v.shape, v.dtype) for v in values),
        in_specs=[pl.BlockSpec(memory_space=pltpu.VMEM)] * 3,
        out_specs=tuple([pl.BlockSpec(memory_space=pl.ANY)] * 3),
        scratch_shapes=[pltpu.SemaphoreType.DMA((3,))],
    )(*values)


def shards(
    projection,
    multiplier,
    reprojection,
    intensity,
    row_start,
    column_start,
    probe_field,
    probe_mask,
    weights,
    ray_blocks,
    ray_counts,
    volume,
):
    return write_out(
        admm_step(
            ray_blocks, ray_counts, row_start, column_start, projection, multiplier, reprojection,
            intensity, probe_field, probe_mask, volume, weights,
        )
    )


def solution(mesh):
    return jax.shard_map(
        shards,
        mesh=mesh,
        in_specs=(
            P(("angle", "half"), None, "tile", None),
            P(("angle", "half"), None, "tile", None),
            P(("angle", "half"), "tile", None),
            P(("angle", "half"), "tile", None, None),
            P(("angle", "half"), "tile"),
            P(("angle", "half"), "tile"),
            P(),
            P(),
            P("angle", None, None, None, None),
            P("angle", None, None),
            P("angle", None),
            P("angle", ("tile", "half"), None),
        ),
        out_specs=(
            P(("angle", "half"), None, "tile", None),
            P("angle", ("tile", "half"), None),
            P("angle", None, ("tile", "half"), None),
        ),
        check_vma=False,
    )
```
